32 devices in a mesh: pipe: 4 (over x, core), seq: 8 (over z, y).
Axes of the slice: x: 2, y: 2, z: 4, core: 2. Of those that a mesh axis runs over, the one named last changes fastest.
Arguments:
- value_in: bfloat16 [4, 1024, 4096], P('pipe', 'seq'), may hold values from -6 to 6
- gate_one: bfloat16 [4, 1024, 4096], P('pipe', 'seq'), may hold values from -6 to 6
- gate_two: bfloat16 [4, 1024, 4096], P('pipe', 'seq'), may hold values from -6 to 6
- out_grad: bfloat16 [4, 1024, 4096], P('pipe', 'seq'), may hold values from -6 to 6
- w_embed: float32 [4, 33, 64], P('pipe'), may hold values from -1 to 1
- b_embed: float32 [4, 64], P('pipe'), may hold values from -4 to 4
- w_filter: float32 [4, 64, 4096], P('pipe', None, 'seq'), may hold values from -0.75 to 0.75
- decay: float32 [4, 4096], P('pipe', 'seq'), may hold values from 0.3 to 128
- skip: float32 [4, 4096], P('pipe', 'seq'), may hold values from -4 to 4
Outputs:
- next_input: bfloat16 [4, 1024, 4096], P('pipe', 'seq')
- grad_value: bfloat16 [4, 1024, 4096], P('pipe', 'seq')
- grad_gate_one: bfloat16 [4, 1024, 4096], P('pipe', 'seq')
- grad_gate_two: bfloat16 [4, 1024, 4096], P('pipe', 'seq')
- grad_w_embed: float32 [4, 33, 64], P('pipe')
- grad_b_embed: float32 [4, 64], P('pipe')
- grad_w_filter: float32 [4, 64, 4096], P('pipe', None, 'seq')
- grad_decay: float32 [4, 4096], P('pipe', 'seq')
- grad_skip: float32 [4, 4096], P('pipe', 'seq')
The draws below stay inside these ranges and needn't reach their ends.
All inputs are finite; a program needn't handle non-finite values.
Results may differ from the reference program's by a relative error of at most 0.0058.
Values may be sent and summed in bfloat16 or wider, within the bound.
A program may use at most 128 MiB of HBM per device.

```python
import math
import jax
import jax.numpy as jnp
from jax import lax

C = 4096
F = 64
E = 33
TOKENS = 1024
SECTIONS = 4


def levels(key, extent, split, low, largest):
    factor_of = 1.0
    for position, shards_of in split:
        draws = jax.random.uniform(jax.random.fold_in(jax.random.fold_in(key, 6), position), (shards_of,), jnp.float32, low / len(split), largest / len(split))
        factor_of = factor_of * jnp.repeat(jnp.exp(draws), extent[position] // shards_of).reshape((-1,) + (1,) * (len(extent) - 1 - position))
    return factor_of


def scatter_about(rng, dims, spread, reach, pieces=(), held_as=jnp.bfloat16):
    values = jax.random.normal(rng, dims, jnp.float32) * spread
    if len(pieces) > 0:
        values = levels(rng, dims, pieces, -0.22, 0.18) * values
    return jnp.clip(values, min=-reach, max=reach).astype(held_as)


def setup_inputs(seed: int = 0) -> dict:
    splits = jax.random.split(jax.random.key(seed), 10)
    value_in = scatter_about(splits[0], (SECTIONS, TOKENS, C), 1.0, 6.0, ((0, 4), (1, 8)))
    gate_one = scatter_about(splits[1], (SECTIONS, TOKENS, C), 1.0, 6.0, ((0, 4), (1, 8)))
    gate_two = scatter_about(splits[2], (SECTIONS, TOKENS, C), 1.0, 6.0, ((0, 4), (1, 8)))
    out_grad = scatter_about(splits[3], (SECTIONS, TOKENS, C), 1.0, 6.0, ((0, 4), (1, 8)))
    w_embed = scatter_about(splits[4], (SECTIONS, E, F), E ** -0.5, 1.0, ((0, 4),), jnp.float32)
    b_embed = scatter_about(splits[5], (SECTIONS, F), 1.0, 4.0, ((0, 4),), jnp.float32)
    w_filter = scatter_about(splits[6], (SECTIONS, F, C), F ** -0.5, 0.75, ((0, 4), (2, 8)), jnp.float32)
    decay = jnp.clip(jnp.exp(math.log(128.0) - 6.056003 * jax.random.uniform(splits[7], (SECTIONS, C), jnp.float32) ** levels(splits[7], (SECTIONS, C), ((0, 4), (1, 8)), -0.2, 0.2)), 0.3, 128.0)
    skip = scatter_about(splits[8], (SECTIONS, C), 1.0, 4.0, ((0, 4), (1, 8)), jnp.float32)
    return {"value_in": value_in, "gate_one": gate_one, "gate_two": gate_two, "out_grad": out_grad, "w_embed": w_embed, "b_embed": b_embed, "w_filter": w_filter, "decay": decay, "skip": skip}


def contract(form, left, right):
    return jnp.einsum(form, left, right, precision=lax.Precision.HIGHEST)

def position_features(length):
    position_ids = jnp.arange(length, dtype=jnp.int32)
    band_count = (E - 1) // 2
    band_index = jnp.arange(1, band_count + 1, dtype=jnp.int32)
    turn_ids = band_index[:, None] * band_index[:, None] * position_ids[None, :] % length
    angles = 2.0 * math.pi / length * turn_ids.astype(jnp.float32)
    position_ramp = position_ids.astype(jnp.float32)[None, :] / length
    return jnp.concatenate([position_ramp, jnp.cos(angles), jnp.sin(angles)], axis=0)

def section(inputs):
    values, gate_first, gate_second, cotangent, embed_w, embed_b, filter_w, decay_rate, skip_w = inputs
    length = values.shape[0]
    width = values.shape[1]
    blocks = 8
    block_width = width // blocks
    fft_total = 2 * length
    features = position_features(length)
    preact = contract('ef,et->ft', embed_w, features) + embed_b[:, None]
    activation = jnp.sin(preact)
    weighted = (values.astype(jnp.float32) * gate_first.astype(jnp.float32)).astype(jnp.bfloat16)
    upstream = (cotangent.astype(jnp.float32) * gate_second.astype(jnp.float32)).astype(jnp.bfloat16)
    positions = jnp.arange(length, dtype=jnp.int32).astype(jnp.float32)[:, None]

    def split_blocks(field):
        return jnp.moveaxis(field.reshape(field.shape[0], blocks, block_width), 1, 0)

    def merge_blocks(field):
        return jnp.moveaxis(field, 0, 1).reshape(field.shape[1], width)

    def one_block(parts):
        weighted_b, upstream_b, filter_b, decay_b, skip_b = parts
        weighted_f = weighted_b.astype(jnp.float32)
        upstream_f = upstream_b.astype(jnp.float32)
        envelope = jnp.exp(-decay_b[None, :] * positions / length) * (1.0 / math.sqrt(length))
        kernel = contract('ft,fc->tc', activation, filter_b) * envelope
        kernel_spec = jnp.fft.rfft(kernel, n=fft_total, axis=0)
        weighted_spec = jnp.fft.rfft(weighted_f, n=fft_total, axis=0)
        upstream_spec = jnp.fft.rfft(upstream_f, n=fft_total, axis=0)
        conv = jnp.fft.irfft(kernel_spec * weighted_spec, n=fft_total, axis=0)[:length]
        mixed_b = (conv + skip_b[None, :] * weighted_f).astype(jnp.bfloat16)
        backward_conv = jnp.fft.irfft(jnp.conj(kernel_spec) * upstream_spec, n=fft_total, axis=0)[:length]
        grad_weighted_b = (backward_conv + skip_b[None, :] * upstream_f).astype(jnp.bfloat16)
        grad_skip_b = lax.optimization_barrier(jnp.sum(upstream_f * weighted_f, axis=0))
        grad_kernel = jnp.fft.irfft(jnp.conj(weighted_spec) * upstream_spec, n=fft_total, axis=0)[:length]
        grad_decay_b = lax.optimization_barrier(jnp.sum(grad_kernel * kernel * (-positions / length), axis=0))
        grad_raw = grad_kernel * envelope
        grad_filter_b = contract('ft,tc->fc', activation, grad_raw)
        grad_act_b = contract('fc,tc->ft', filter_b, grad_raw)
        return (mixed_b, grad_weighted_b, grad_skip_b, grad_decay_b, grad_filter_b, grad_act_b)
    filter_blocks = jnp.moveaxis(filter_w.reshape(F, blocks, block_width), 1, 0)
    mixed_all, grad_weighted_all, skip_all, decay_all, filter_all, act_all = lax.map(one_block, (split_blocks(weighted), split_blocks(upstream), filter_blocks, decay_rate.reshape(blocks, block_width), skip_w.reshape(blocks, block_width)))
    mixed = merge_blocks(mixed_all)
    grad_weighted = merge_blocks(grad_weighted_all)
    grad_preact = lax.optimization_barrier(jnp.sum(act_all, axis=0)) * jnp.cos(preact)
    grad_embed_w = contract('et,ft->ef', features, grad_preact)
    grad_embed_b = lax.optimization_barrier(jnp.sum(grad_preact, axis=1))
    grad_filter_w = jnp.moveaxis(filter_all, 0, 1).reshape(F, width)
    output = (gate_second.astype(jnp.float32) * mixed.astype(jnp.float32)).astype(jnp.bfloat16)
    grad_values = (grad_weighted.astype(jnp.float32) * gate_first.astype(jnp.float32)).astype(jnp.bfloat16)
    grad_first = (grad_weighted.astype(jnp.float32) * values.astype(jnp.float32)).astype(jnp.bfloat16)
    grad_second = (cotangent.astype(jnp.float32) * mixed.astype(jnp.float32)).astype(jnp.bfloat16)
    return (output, grad_values, grad_first, grad_second, grad_embed_w, grad_embed_b, grad_filter_w, decay_all.reshape(width), skip_all.reshape(width))

def reference(value_in, gate_one, gate_two, out_grad, w_embed, b_embed, w_filter, decay, skip):
    results = lax.map(section, (value_in, gate_one, gate_two, out_grad, w_embed, b_embed, w_filter, decay, skip))
    output, grad_values, grad_first, grad_second, grad_embed_w, grad_embed_b, grad_filter_w, grad_decay, grad_skip = results
    next_input = jnp.roll(output, 1, axis=0)
    grad_value = jnp.roll(grad_values, -1, axis=0)
    grad_gate_one = jnp.roll(grad_first, -1, axis=0)
    grad_gate_two = jnp.roll(grad_second, -1, axis=0)
    return (next_input, grad_value, grad_gate_one, grad_gate_two, grad_embed_w, grad_embed_b, grad_filter_w, grad_decay, grad_skip)
```

```python
import math

import jax
import jax.numpy as jnp
from jax import lax
from jax.sharding import PartitionSpec as P

E = 33


def from_behind(value, axis, steps):
    count = lax.axis_size(axis)
    pairs = [(source, (source + steps) % count) for source in range(count)]
    return lax.ppermute(value, axis, pairs)


def contract(form, left, right):
    return jnp.einsum(form, left, right, precision=lax.Precision.HIGHEST)


def position_features(length):
    position_ids = jnp.arange(length, dtype=jnp.int32)
    band_count = (E - 1) // 2
    band_index = jnp.arange(1, band_count + 1, dtype=jnp.int32)
    turn_ids = band_index[:, None] * band_index[:, None] * position_ids[None, :] % length
    angles = 2.0 * math.pi / length * turn_ids.astype(jnp.float32)
    position_ramp = position_ids.astype(jnp.float32)[None, :] / length
    return jnp.concatenate([position_ramp, jnp.cos(angles), jnp.sin(angles)], axis=0)


def build_tables(length):
    fft_total = 2 * length
    outer_len = 128
    half_len = outer_len // 2
    kept_len = half_len + 1
    inner_len = fft_total // outer_len
    index_kept = jnp.arange(kept_len, dtype=jnp.int32)
    index_half = jnp.arange(half_len, dtype=jnp.int32)
    index_inner = jnp.arange(inner_len, dtype=jnp.int32)
    angle_outer = (
        2.0
        * math.pi
        / outer_len
        * (index_kept[:, None] * index_half[None, :] % outer_len).astype(jnp.float32)
    )
    cos_outer = jnp.cos(angle_outer)
    sin_outer = jnp.sin(angle_outer)
    table_first = jnp.concatenate([cos_outer, -sin_outer], axis=0)
    angle_twist = (
        2.0
        * math.pi
        / fft_total
        * (index_kept[:, None] * index_inner[None, :] % fft_total).astype(jnp.float32)
    )
    cos_twist = jnp.cos(angle_twist)[:, :, None]
    sin_twist = jnp.sin(angle_twist)[:, :, None]
    angle_inner = (
        2.0
        * math.pi
        / inner_len
        * (index_inner[:, None] * index_inner[None, :] % inner_len).astype(jnp.float32)
    )
    cos_inner = jnp.cos(angle_inner)
    sin_inner = jnp.sin(angle_inner)
    table_second = jnp.stack(
        [jnp.stack([cos_inner, sin_inner], axis=1), jnp.stack([-sin_inner, cos_inner], axis=1)],
        axis=0,
    )
    table_back = jnp.stack(
        [jnp.stack([cos_inner, -sin_inner], axis=1), jnp.stack([sin_inner, cos_inner], axis=1)],
        axis=0,
    )
    weight_kept = (
        jnp.where((index_kept == 0) | (index_kept == half_len), 1.0, 2.0).astype(jnp.float32)
        / fft_total
    )
    table_last = jnp.stack(
        [
            jnp.transpose(cos_outer) * weight_kept[None, :],
            -jnp.transpose(sin_outer) * weight_kept[None, :],
        ],
        axis=1,
    )
    return (
        table_first,
        cos_twist,
        sin_twist,
        table_second,
        table_back,
        table_last,
        half_len,
        kept_len,
        inner_len,
    )


def staged_forward(field, tables_all):
    (
        table_first,
        cos_twist,
        sin_twist,
        table_second,
        table_back,
        table_last,
        half_len,
        kept_len,
        inner_len,
    ) = tables_all
    columns = field.shape[1]
    shaped = field.reshape(half_len, inner_len, columns)
    stacked = contract("kn,npc->kpc", table_first, shaped)
    part_re = stacked[:kept_len]
    part_im = stacked[kept_len:]
    twisted = jnp.stack(
        [part_re * cos_twist + part_im * sin_twist, part_im * cos_twist - part_re * sin_twist],
        axis=0,
    )
    return contract("sqrp,rkpc->skqc", table_second, twisted)


def staged_inverse(spec, tables_all):
    (
        table_first,
        cos_twist,
        sin_twist,
        table_second,
        table_back,
        table_last,
        half_len,
        kept_len,
        inner_len,
    ) = tables_all
    columns = spec.shape[3]
    sectioned = contract("sprq,rkqc->skpc", table_back, spec)
    section_re = sectioned[0]
    section_im = sectioned[1]
    twisted = jnp.stack(
        [
            section_re * cos_twist - section_im * sin_twist,
            section_im * cos_twist + section_re * sin_twist,
        ],
        axis=0,
    )
    result = contract("nrk,rkpc->npc", table_last, twisted)
    return result.reshape(half_len * inner_len, columns)


def dense_tables(length):
    block = 128
    fine = jnp.arange(block, dtype=jnp.int32)
    coarse = jnp.arange(length // block, dtype=jnp.int32) * block
    point = jnp.arange(length, dtype=jnp.int32)
    unit = math.pi / (2 * length)

    def pair(count):
        angle = unit * (count % (4 * length)).astype(jnp.float32)
        return jnp.cos(angle), jnp.sin(angle)

    def joined(first, second):
        (cos_f, sin_f), (cos_s, sin_s) = first, second
        cos_j = cos_s[:, None, :] * cos_f[None] - sin_s[:, None, :] * sin_f[None]
        sin_j = sin_s[:, None, :] * cos_f[None] + cos_s[:, None, :] * sin_f[None]
        return cos_j.reshape(length, length), sin_j.reshape(length, length)

    odd = 2 * point + 1
    cos_k, sin_k = joined(
        pair((2 * fine + 1)[:, None] * point[None, :]),
        pair((2 * coarse)[:, None] * point[None, :]),
    )
    ahead = jnp.concatenate([cos_k, -sin_k], axis=0).astype(jnp.bfloat16)
    cos_n, sin_n = joined(
        pair(fine[:, None] * odd[None, :]), pair(coarse[:, None] * odd[None, :])
    )
    back = (jnp.concatenate([cos_n, -sin_n], axis=1) * (1.0 / length)).astype(jnp.bfloat16)
    return ahead, back


def dense_forward(field, tables_all):
    spec = jnp.dot(tables_all[0], field.astype(jnp.bfloat16), preferred_element_type=jnp.float32)
    return spec.reshape(2, field.shape[0], field.shape[1])


def dense_inverse(spec, tables_all):
    flat = spec.reshape(2 * spec.shape[1], spec.shape[2])
    return jnp.dot(tables_all[1], flat.astype(jnp.bfloat16), preferred_element_type=jnp.float32)


def spectral_product(left, right, conjugate_left):
    left_re = left[0]
    left_im = left[1]
    right_re = right[0]
    right_im = right[1]
    if conjugate_left:
        left_im = -left_im
    return jnp.stack(
        [left_re * right_re - left_im * right_im, left_re * right_im + left_im * right_re], axis=0
    )


def per_device(value_in, gate_one, gate_two, out_grad, w_embed, b_embed, w_filter, decay, skip):
    values = value_in[0]
    gate_first = gate_one[0]
    gate_second = gate_two[0]
    cotangent = out_grad[0]
    filter_w = w_filter[0]
    shards = lax.axis_size("seq")
    length = values.shape[0] * shards
    weighted = (values.astype(jnp.float32) * gate_first.astype(jnp.float32)).astype(jnp.bfloat16)
    upstream = (cotangent.astype(jnp.float32) * gate_second.astype(jnp.float32)).astype(
        jnp.bfloat16
    )
    features = position_features(length)
    preact = contract("ef,et->ft", w_embed[0], features) + b_embed[0][:, None]
    activation = jnp.sin(preact)
    positions = jnp.arange(length, dtype=jnp.int32).astype(jnp.float32)[:, None]
    envelope = jnp.exp(-decay[0][None, :] * positions / length) * (1.0 / math.sqrt(length))
    kernel = contract("ft,fc->tc", activation, filter_w) * envelope
    if length <= 1024 and length % 128 == 0:
        tables_all = dense_tables(length)
        forward_transform, inverse_transform = dense_forward, dense_inverse
    else:
        tables_all = build_tables(length)
        forward_transform, inverse_transform = staged_forward, staged_inverse
    kernel_spec = forward_transform(kernel, tables_all)
    skip_row = skip[0][None, :]
    weighted_chan, upstream_chan = (
        lax.all_to_all(weighted, "seq", split_axis=1, concat_axis=0, tiled=True),
        lax.all_to_all(upstream, "seq", split_axis=1, concat_axis=0, tiled=True),
    )
    weighted_f = weighted_chan.astype(jnp.float32)
    weighted_spec = forward_transform(weighted_f, tables_all)
    conv = inverse_transform(spectral_product(kernel_spec, weighted_spec, False), tables_all)
    mixed_chan, weighted_f, weighted_spec = (
        (conv + skip_row * weighted_f).astype(jnp.bfloat16),
        weighted_f,
        weighted_spec,
    )
    upstream_f = upstream_chan.astype(jnp.float32)
    upstream_spec = forward_transform(upstream_f, tables_all)
    backward_conv = inverse_transform(
        spectral_product(kernel_spec, upstream_spec, True), tables_all
    )
    grad_chan = (backward_conv + skip_row * upstream_f).astype(jnp.bfloat16)
    grad_skip = jnp.sum(upstream_f * weighted_f, axis=0)
    grad_kernel = inverse_transform(
        spectral_product(weighted_spec, upstream_spec, True), tables_all
    )
    grad_chan, grad_skip, grad_kernel = (grad_chan, grad_skip, grad_kernel)
    mixed_seq, grad_weighted = (
        lax.all_to_all(mixed_chan, "seq", split_axis=0, concat_axis=1, tiled=True),
        lax.all_to_all(grad_chan, "seq", split_axis=0, concat_axis=1, tiled=True),
    )
    output = (gate_second.astype(jnp.float32) * mixed_seq.astype(jnp.float32)).astype(jnp.bfloat16)
    next_input = from_behind(output, "pipe", 1)
    grad_decay = jnp.sum(grad_kernel * kernel * (-positions / length), axis=0)
    grad_raw = grad_kernel * envelope
    grad_filter_w = contract("ft,tc->fc", activation, grad_raw)
    grad_preact = contract("fc,tc->ft", filter_w, grad_raw) * jnp.cos(preact)
    part_weight = contract("et,ft->ef", features, grad_preact)
    part_bias = jnp.sum(grad_preact, axis=1)
    grad_embed_w, grad_embed_b = lax.psum((part_weight, part_bias), "seq")
    grad_values = (grad_weighted.astype(jnp.float32) * gate_first.astype(jnp.float32)).astype(
        jnp.bfloat16
    )
    grad_first = (grad_weighted.astype(jnp.float32) * values.astype(jnp.float32)).astype(
        jnp.bfloat16
    )
    grad_second = (cotangent.astype(jnp.float32) * mixed_seq.astype(jnp.float32)).astype(
        jnp.bfloat16
    )
    moved_values, moved_first, moved_second = from_behind(
        (grad_values, grad_first, grad_second), "pipe", -1
    )
    return (
        next_input[None],
        moved_values[None],
        moved_first[None],
        moved_second[None],
        grad_embed_w[None],
        grad_embed_b[None],
        grad_filter_w[None],
        grad_decay[None],
        grad_skip[None],
    )


def solution(mesh):
    return jax.shard_map(
        per_device,
        mesh=mesh,
        in_specs=(
            P("pipe", "seq", None),
            P("pipe", "seq", None),
            P("pipe", "seq", None),
            P("pipe", "seq", None),
            P("pipe", None, None),
            P("pipe", None),
            P("pipe", None, "seq"),
            P("pipe", "seq"),
            P("pipe", "seq"),
        ),
        out_specs=(
            P("pipe", "seq", None),
            P("pipe", "seq", None),
            P("pipe", "seq", None),
            P("pipe", "seq", None),
            P("pipe", None, None),
            P("pipe", None),
            P("pipe", None, "seq"),
            P("pipe", "seq"),
            P("pipe", "seq"),
        ),
        check_vma=False,
    )
```

```python
import functools
import math

import jax
import jax.numpy as jnp
import numpy as np
from jax import lax
from jax.experimental import pallas as pl
from jax.experimental.pallas import tpu as pltpu
from jax.sharding import PartitionSpec as P

E = 33


def from_behind(value, axis, steps):
    count = lax.axis_size(axis)
    pairs = [(source, (source + steps) % count) for source in range(count)]
    return lax.ppermute(value, axis, pairs)


def contract(form, left, right):
    return jnp.einsum(form, left, right, precision=lax.Precision.HIGHEST)


def position_features(length):
    position_ids = jnp.arange(length, dtype=jnp.int32)
    band_count = (E - 1) // 2
    band_index = jnp.arange(1, band_count + 1, dtype=jnp.int32)
    turn_ids = band_index[:, None] * band_index[:, None] * position_ids[None, :] % length
    angles = 2.0 * math.pi / length * turn_ids.astype(jnp.float32)
    position_ramp = position_ids.astype(jnp.float32)[None, :] / length
    return jnp.concatenate([position_ramp, jnp.cos(angles), jnp.sin(angles)], axis=0)


def build_tables(length):
    fft_total = 2 * length
    outer_len = 128
    half_len = outer_len // 2
    kept_len = half_len + 1
    inner_len = fft_total // outer_len
    index_kept = jnp.arange(kept_len, dtype=jnp.int32)
    index_half = jnp.arange(half_len, dtype=jnp.int32)
    index_inner = jnp.arange(inner_len, dtype=jnp.int32)
    angle_outer = (
        2.0
        * math.pi
        / outer_len
        * (index_kept[:, None] * index_half[None, :] % outer_len).astype(jnp.float32)
    )
    cos_outer = jnp.cos(angle_outer)
    sin_outer = jnp.sin(angle_outer)
    table_first = jnp.concatenate([cos_outer, -sin_outer], axis=0)
    angle_twist = (
        2.0
        * math.pi
        / fft_total
        * (index_kept[:, None] * index_inner[None, :] % fft_total).astype(jnp.float32)
    )
    cos_twist = jnp.cos(angle_twist)[:, :, None]
    sin_twist = jnp.sin(angle_twist)[:, :, None]
    angle_inner = (
        2.0
        * math.pi
        / inner_len
        * (index_inner[:, None] * index_inner[None, :] % inner_len).astype(jnp.float32)
    )
    cos_inner = jnp.cos(angle_inner)
    sin_inner = jnp.sin(angle_inner)
    table_second = jnp.stack(
        [jnp.stack([cos_inner, sin_inner], axis=1), jnp.stack([-sin_inner, cos_inner], axis=1)],
        axis=0,
    )
    table_back = jnp.stack(
        [jnp.stack([cos_inner, -sin_inner], axis=1), jnp.stack([sin_inner, cos_inner], axis=1)],
        axis=0,
    )
    weight_kept = (
        jnp.where((index_kept == 0) | (index_kept == half_len), 1.0, 2.0).astype(jnp.float32)
        / fft_total
    )
    table_last = jnp.stack(
        [
            jnp.transpose(cos_outer) * weight_kept[None, :],
            -jnp.transpose(sin_outer) * weight_kept[None, :],
        ],
        axis=1,
    )
    return (
        table_first,
        cos_twist,
        sin_twist,
        table_second,
        table_back,
        table_last,
        half_len,
        kept_len,
        inner_len,
    )


def staged_forward(field, tables_all):
    (
        table_first,
        cos_twist,
        sin_twist,
        table_second,
        table_back,
        table_last,
        half_len,
        kept_len,
        inner_len,
    ) = tables_all
    columns = field.shape[1]
    shaped = field.reshape(half_len, inner_len, columns)
    stacked = contract("kn,npc->kpc", table_first, shaped)
    part_re = stacked[:kept_len]
    part_im = stacked[kept_len:]
    twisted = jnp.stack(
        [part_re * cos_twist + part_im * sin_twist, part_im * cos_twist - part_re * sin_twist],
        axis=0,
    )
    return contract("sqrp,rkpc->skqc", table_second, twisted)


def staged_inverse(spec, tables_all):
    (
        table_first,
        cos_twist,
        sin_twist,
        table_second,
        table_back,
        table_last,
        half_len,
        kept_len,
        inner_len,
    ) = tables_all
    columns = spec.shape[3]
    sectioned = contract("sprq,rkqc->skpc", table_back, spec)
    section_re = sectioned[0]
    section_im = sectioned[1]
    twisted = jnp.stack(
        [
            section_re * cos_twist - section_im * sin_twist,
            section_im * cos_twist + section_re * sin_twist,
        ],
        axis=0,
    )
    result = contract("nrk,rkpc->npc", table_last, twisted)
    return result.reshape(half_len * inner_len, columns)


ROWS = 128
PAIR = 2 * ROWS
PADDED = 40


def split_tables(length):
    blocks = length // ROWS
    fine = np.arange(ROWS)
    coarse = np.arange(blocks) * ROWS
    point = np.arange(length)
    unit = math.pi / (2 * length)

    def pair(count, scale=1.0):
        angle = unit * (count % (4 * length))
        return [
            jnp.asarray((np.cos(angle) * scale).astype(np.float32)),
            jnp.asarray((np.sin(angle) * scale).astype(np.float32)),
        ]

    odd = 2 * point + 1
    ahead = pair((2 * fine + 1)[:, None] * point[None]) + pair((2 * coarse)[:, None] * point[None])
    back = pair(fine[:, None] * odd[None], 1.0 / length) + pair(coarse[:, None] * odd[None])
    return ahead + back


def padded_features(length):
    position = np.arange(length)
    band = np.arange(1, (E - 1) // 2 + 1)
    angle = 2.0 * math.pi / length * ((band[:, None] ** 2 * position[None]) % length)
    table = np.zeros((PADDED, length), np.float32)
    table[0] = position / length
    table[1 : 1 + len(band)] = np.cos(angle)
    table[1 + len(band) : E] = np.sin(angle)
    table[E] = 1.0
    return table


def section_kernel(
    shards, pipes,
    v, g1, g2, og, wf, decay, skip, wext, wext_t, feat, feat_t,
    dc, ds, ec, es, bc, bs, ac, asn,
    o_next, o_val, o_first, o_second, o_emb, o_wf, o_decay, o_skip,
    ahead, back, kb, kf, env, kspec, wspec, prod, corr, graw,
    wsend, usend, wch, uch, mch, gch, mseq, gseq, stage, part, parts,
    a_send, a_recv, p_send, p_recv, x_send, x_recv,
):
    f32, bf16 = jnp.float32, jnp.bfloat16
    length = shards * ROWS
    width = wf.shape[1]
    pipe = lax.axis_index("pipe")
    me = lax.axis_index("seq")
    mine = me // 2
    partner = me + 1 - 2 * (me % 2)
    pairs = shards // 2
    nxt = (pipe + 1) % pipes
    prv = (pipe + pipes - 1) % pipes
    high = lax.Precision.HIGHEST

    def peer(step, sign):
        far = 1 + step // 2
        return ((mine + sign * far + pairs) % pairs) * 2 + step % 2

    def others(sign, visit):
        def body(step, carry):
            visit(peer(step, sign))
            return carry

        lax.fori_loop(0, shards - 2, body, 0)
        visit(partner)

    def rows(index):
        return pl.ds(pl.multiple_of(index * ROWS, ROWS), ROWS)

    def cols(index):
        return pl.ds(pl.multiple_of(index * width, width), width)

    def wide(index):
        return pl.ds(pl.multiple_of(index * PAIR, PAIR), PAIR)

    def exchange(kind, src, dst, there, source):
        return pltpu.make_async_remote_copy(
            src_ref=src, dst_ref=dst, send_sem=a_send.at[kind, there],
            recv_sem=a_recv.at[kind, source], device_id=(pipe, there),
            device_id_type=pl.DeviceIdType.MESH,
        )

    def handed(kind, slot):
        out = (o_next, o_second, o_val, o_first)[kind]
        return pltpu.make_async_remote_copy(
            src_ref=stage.at[kind, slot], dst_ref=out.at[:, cols(slot)],
            send_sem=p_send.at[kind, slot], recv_sem=p_recv.at[kind, slot],
            device_id=(nxt if kind == 0 else prv, me),
            device_id_type=pl.DeviceIdType.MESH,
        )

    def shared(there, source):
        return pltpu.make_async_remote_copy(
            src_ref=part, dst_ref=parts.at[source], send_sem=x_send.at[there],
            recv_sem=x_recv.at[source], device_id=(pipe, there),
            device_id_type=pl.DeviceIdType.MESH,
        )

    def times(one, two, index):
        return (one[:, cols(index)].astype(f32) * two[:, cols(index)].astype(f32)).astype(bf16)

    barrier = pltpu.get_barrier_semaphore()

    def greet(there):
        pl.semaphore_signal(
            barrier, inc=1, device_id=(pipe, there), device_id_type=pl.DeviceIdType.MESH
        )

    others(1, greet)
    for side in (nxt, prv):
        pl.semaphore_signal(
            barrier, inc=1, device_id=(side, me), device_id_type=pl.DeviceIdType.MESH
        )
    pl.semaphore_wait(barrier, shards + 1)

    def send_weighted(there):
        wsend[there] = times(v, g1, there)
        exchange(0, wsend.at[there], wch.at[rows(me), :], there, me).start()

    others(1, send_weighted)
    wch[rows(me), :] = times(v, g1, me)

    def make_kernel(tile, carry):
        here = wide(tile)
        step = (lax.broadcasted_iota(jnp.int32, (PAIR, 1), 0) + tile * PAIR).astype(f32)
        act = jnp.sin(jnp.dot(feat_t[here, :], wext[...], precision=high))
        envelope = jnp.exp(-decay[...] * step / length) * (1.0 / math.sqrt(length))
        kernel = jnp.dot(act, wf[...], precision=high) * envelope
        env[here, :] = envelope
        kf[here, :] = kernel
        kb[here, :] = kernel.astype(bf16)
        return carry

    lax.fori_loop(0, length // PAIR, make_kernel, 0)

    def make_ahead(tile, carry):
        row_c, row_s = ec[pl.ds(tile, 1), :], es[pl.ds(tile, 1), :]
        base = pl.multiple_of(tile * PAIR, PAIR)
        ahead[pl.ds(base, ROWS), :] = (dc[...] * row_c - ds[...] * row_s).astype(bf16)
        ahead[pl.ds(base + ROWS, ROWS), :] = (-(ds[...] * row_c + dc[...] * row_s)).astype(bf16)
        return carry

    lax.fori_loop(0, shards, make_ahead, 0)

    def make_kspec(tile, carry):
        kspec[wide(tile), :] = jnp.dot(
            ahead[wide(tile), :], kb[...], preferred_element_type=f32
        )
        return carry

    lax.fori_loop(0, shards, make_kspec, 0)

    def send_upstream(there):
        usend[there] = times(og, g2, there)
        exchange(1, usend.at[there], uch.at[rows(me), :], there, me).start()

    others(1, send_upstream)
    uch[rows(me), :] = times(og, g2, me)

    def make_back(tile, carry):
        full_c, full_s = ac[pl.ds(tile, 1), :], asn[pl.ds(tile, 1), :]
        for block in range(shards):
            lanes = slice(block * ROWS, (block + 1) * ROWS)
            row_c, row_s = full_c[:, lanes], full_s[:, lanes]
            cos_b, sin_b = bc[:, lanes], bs[:, lanes]
            start = block * PAIR
            back[rows(tile), start : start + ROWS] = (cos_b * row_c - sin_b * row_s).astype(bf16)
            back[rows(tile), start + ROWS : start + PAIR] = (
                -(sin_b * row_c + cos_b * row_s)
            ).astype(bf16)
        return carry

    lax.fori_loop(0, shards, make_back, 0)

    others(-1, lambda source: exchange(
        0, wsend.at[source], wch.at[rows(source), :], source, source).wait_recv())

    def make_product(tile, carry):
        here = wide(tile)
        spec = jnp.dot(ahead[here, :], wch[...], preferred_element_type=f32)
        wspec[here, :] = spec
        k_re, k_im = kspec[here, :][:ROWS], kspec[here, :][ROWS:]
        x_re, x_im = spec[:ROWS], spec[ROWS:]
        prod[here, :] = jnp.concatenate(
            [k_re * x_re - k_im * x_im, k_re * x_im + k_im * x_re], axis=0
        ).astype(bf16)
        return carry

    lax.fori_loop(0, shards, make_product, 0)

    def convolved(kind, field, result, landing):
        def chunk(index):
            here = wide(index)
            conv = jnp.dot(back[here, :], prod[...], preferred_element_type=f32)
            result[here, :] = (conv + skip[...] * field[here, :].astype(f32)).astype(bf16)

        def far(step, carry):
            index = (mine + 1 + step) % pairs
            chunk(index)
            for side in range(2):
                there = index * 2 + side
                exchange(kind, result.at[rows(there), :], landing.at[me], there, me).start()
            return carry

        lax.fori_loop(0, pairs - 1, far, 0)
        chunk(mine)
        exchange(kind, result.at[rows(partner), :], landing.at[me], partner, me).start()
        landing[me] = result[rows(me), :]

    convolved(2, wch, mch, mseq)

    others(-1, lambda source: exchange(
        1, usend.at[source], uch.at[rows(source), :], source, source).wait_recv())

    def make_products(tile, carry):
        here = wide(tile)
        spec = jnp.dot(ahead[here, :], uch[...], preferred_element_type=f32)
        x_re, x_im = spec[:ROWS], spec[ROWS:]
        for left, target in ((kspec, prod), (wspec, corr)):
            l_re, l_im = left[here, :][:ROWS], left[here, :][ROWS:]
            target[here, :] = jnp.concatenate(
                [l_re * x_re + l_im * x_im, l_re * x_im - l_im * x_re], axis=0
            ).astype(bf16)
        return carry

    lax.fori_loop(0, shards, make_products, 0)
    convolved(3, uch, gch, gseq)

    def pass_mixed(source):
        block = mseq[source].astype(f32)
        stage[0, source] = (g2[:, cols(source)].astype(f32) * block).astype(bf16)
        stage[1, source] = (og[:, cols(source)].astype(f32) * block).astype(bf16)
        handed(0, source).start()
        handed(1, source).start()

    def land_mixed(source):
        exchange(2, mch.at[rows(source), :], mseq.at[source], source, source).wait_recv()
        pass_mixed(source)

    pass_mixed(me)
    others(-1, land_mixed)

    def correlate(tile, carry):
        here = wide(tile)
        step = (lax.broadcasted_iota(jnp.int32, (PAIR, 1), 0) + tile * PAIR).astype(f32)
        grad = jnp.dot(back[here, :], corr[...], preferred_element_type=f32)
        graw[here, :] = (grad * env[here, :]).astype(bf16)
        sum_d, sum_s = carry
        sum_d += jnp.sum(grad * kf[here, :] * (-step / length), axis=0, keepdims=True)
        both = uch[here, :].astype(f32) * wch[here, :].astype(f32)
        return sum_d, sum_s + jnp.sum(both, axis=0, keepdims=True)

    empty = jnp.zeros((1, width), f32)
    sum_d, sum_s = lax.fori_loop(0, length // PAIR, correlate, (empty, empty))
    o_decay[...] = sum_d
    o_skip[...] = sum_s

    def halves(value):
        top = value.astype(bf16)
        return jnp.concatenate([top, (value - top.astype(f32)).astype(bf16)], axis=0)

    hidden = wext_t.shape[0]
    preact = jnp.dot(wext_t[...], feat[...], precision=high)
    both = jnp.dot(halves(jnp.sin(preact)), graw[...], preferred_element_type=f32)
    o_wf[...] = both[:hidden] + both[hidden:]
    both = lax.dot_general(
        halves(wf[...]), graw[...], (((1,), (1,)), ((), ())), preferred_element_type=f32
    )
    grad_pre = (both[:hidden] + both[hidden:]) * jnp.cos(preact)
    part[...] = lax.dot_general(
        feat[...], jnp.concatenate([grad_pre, jnp.zeros_like(grad_pre)], axis=0),
        (((1,), (1,)), ((), ())), precision=high,
    )
    others(1, lambda there: shared(there, me).start())

    def pass_grad(source):
        block = gseq[source].astype(f32)
        stage[2, source] = (g1[:, cols(source)].astype(f32) * block).astype(bf16)
        stage[3, source] = (v[:, cols(source)].astype(f32) * block).astype(bf16)
        handed(2, source).start()
        handed(3, source).start()

    def land_grad(source):
        exchange(3, gch.at[rows(source), :], gseq.at[source], source, source).wait_recv()
        pass_grad(source)

    pass_grad(me)
    others(-1, land_grad)

    parts[me] = part[...]
    others(-1, lambda source: shared(source, source).wait_recv())
    total = parts[0]
    for index in range(1, shards):
        total = total + parts[index]
    o_emb[...] = total

    def sent(there):
        exchange(0, wsend.at[there], wch.at[rows(me), :], there, me).wait_send()
        exchange(1, usend.at[there], uch.at[rows(me), :], there, me).wait_send()
        exchange(2, mch.at[rows(there), :], mseq.at[me], there, me).wait_send()
        exchange(3, gch.at[rows(there), :], gseq.at[me], there, me).wait_send()
        shared(there, me).wait_send()

    others(1, sent)

    def finish(slot, carry):
        for kind in range(4):
            handed(kind, slot).wait()
        return carry

    lax.fori_loop(0, shards, finish, 0)


def fused_section(v, g1, g2, og, w_embed, b_embed, wf, decay, skip):
    shards = lax.axis_size("seq")
    pipes = lax.axis_size("pipe")
    length = shards * ROWS
    wide_cols = v.shape[1]
    width = wf.shape[1]
    hidden = wf.shape[0]
    f32, bf16 = jnp.float32, jnp.bfloat16
    wext = jnp.concatenate(
        [w_embed, b_embed[None], jnp.zeros((PADDED - E - 1, hidden), f32)], axis=0
    )
    feat = padded_features(length)
    tables = split_tables(length)
    vmem = pl.BlockSpec(memory_space=pltpu.VMEM)
    hbm = pl.BlockSpec(memory_space=pl.ANY)
    stream = jax.ShapeDtypeStruct((ROWS, wide_cols), bf16)
    row = jax.ShapeDtypeStruct((1, width), f32)
    dma = pltpu.SemaphoreType.DMA
    results = pl.pallas_call(
        functools.partial(section_kernel, shards, pipes),
        out_shape=(
            stream, stream, stream, stream,
            jax.ShapeDtypeStruct((PADDED, 2 * hidden), f32),
            jax.ShapeDtypeStruct((hidden, width), f32), row, row,
        ),
        in_specs=[vmem] * 19,
        out_specs=(hbm,) * 4 + (vmem,) * 4,
        scratch_shapes=[
            pltpu.VMEM((2 * length, length), bf16),
            pltpu.VMEM((length, 2 * length), bf16),
            pltpu.VMEM((length, width), bf16),
            pltpu.VMEM((length, width), f32),
            pltpu.VMEM((length, width), f32),
            pltpu.VMEM((2 * length, width), f32),
            pltpu.VMEM((2 * length, width), f32),
            pltpu.VMEM((2 * length, width), bf16),
            pltpu.VMEM((2 * length, width), bf16),
            pltpu.VMEM((length, width), bf16),
            pltpu.VMEM((shards, ROWS, width), bf16),
            pltpu.VMEM((shards, ROWS, width), bf16),
            pltpu.VMEM((length, width), bf16),
            pltpu.VMEM((length, width), bf16),
            pltpu.VMEM((length, width), bf16),
            pltpu.VMEM((length, width), bf16),
            pltpu.VMEM((shards, ROWS, width), bf16),
            pltpu.VMEM((shards, ROWS, width), bf16),
            pltpu.VMEM((4, shards, ROWS, width), bf16),
            pltpu.VMEM((PADDED, 2 * hidden), f32),
            pltpu.VMEM((shards, PADDED, 2 * hidden), f32),
            dma((4, shards)), dma((4, shards)),
            dma((4, shards)), dma((4, shards)),
            dma((shards,)), dma((shards,)),
        ],
        compiler_params=pltpu.CompilerParams(
            collective_id=0, has_side_effects=True, vmem_limit_bytes=60 * 1024 * 1024
        ),
    )(
        v, g1, g2, og, wf, decay[None], skip[None], wext, wext.T,
        jnp.asarray(feat), jnp.asarray(feat.T.copy()), *tables,
    )
    moved_next, moved_val, moved_first, moved_second, emb, grad_wf, grad_d, grad_s = results
    return (
        moved_next[None], moved_val[None], moved_first[None], moved_second[None],
        emb[None, :E, :hidden], emb[None, E, :hidden], grad_wf[None], grad_d, grad_s,
    )


def spectral_product(left, right, conjugate_left):
    left_re = left[0]
    left_im = left[1]
    right_re = right[0]
    right_im = right[1]
    if conjugate_left:
        left_im = -left_im
    return jnp.stack(
        [left_re * right_re - left_im * right_im, left_re * right_im + left_im * right_re], axis=0
    )


def per_device(value_in, gate_one, gate_two, out_grad, w_embed, b_embed, w_filter, decay, skip):
    values = value_in[0]
    gate_first = gate_one[0]
    gate_second = gate_two[0]
    cotangent = out_grad[0]
    filter_w = w_filter[0]
    shards = lax.axis_size("seq")
    length = values.shape[0] * shards
    if length <= 1024 and values.shape[0] == ROWS and shards % 2 == 0 and lax.axis_size("pipe") > 2:
        return fused_section(
            values, gate_first, gate_second, cotangent,
            w_embed[0], b_embed[0], filter_w, decay[0], skip[0],
        )
    weighted = (values.astype(jnp.float32) * gate_first.astype(jnp.float32)).astype(jnp.bfloat16)
    upstream = (cotangent.astype(jnp.float32) * gate_second.astype(jnp.float32)).astype(
        jnp.bfloat16
    )
    features = position_features(length)
    preact = contract("ef,et->ft", w_embed[0], features) + b_embed[0][:, None]
    activation = jnp.sin(preact)
    positions = jnp.arange(length, dtype=jnp.int32).astype(jnp.float32)[:, None]
    envelope = jnp.exp(-decay[0][None, :] * positions / length) * (1.0 / math.sqrt(length))
    kernel = contract("ft,fc->tc", activation, filter_w) * envelope
    tables_all = build_tables(length)
    forward_transform, inverse_transform = staged_forward, staged_inverse
    kernel_spec = forward_transform(kernel, tables_all)
    skip_row = skip[0][None, :]
    weighted_chan, upstream_chan = (
        lax.all_to_all(weighted, "seq", split_axis=1, concat_axis=0, tiled=True),
        lax.all_to_all(upstream, "seq", split_axis=1, concat_axis=0, tiled=True),
    )
    weighted_f = weighted_chan.astype(jnp.float32)
    weighted_spec = forward_transform(weighted_f, tables_all)
    conv = inverse_transform(spectral_product(kernel_spec, weighted_spec, False), tables_all)
    mixed_chan, weighted_f, weighted_spec = (
        (conv + skip_row * weighted_f).astype(jnp.bfloat16),
        weighted_f,
        weighted_spec,
    )
    upstream_f = upstream_chan.astype(jnp.float32)
    upstream_spec = forward_transform(upstream_f, tables_all)
    backward_conv = inverse_transform(
        spectral_product(kernel_spec, upstream_spec, True), tables_all
    )
    grad_chan = (backward_conv + skip_row * upstream_f).astype(jnp.bfloat16)
    grad_skip = jnp.sum(upstream_f * weighted_f, axis=0)
    grad_kernel = inverse_transform(
        spectral_product(weighted_spec, upstream_spec, True), tables_all
    )
    grad_chan, grad_skip, grad_kernel = (grad_chan, grad_skip, grad_kernel)
    mixed_seq, grad_weighted = (
        lax.all_to_all(mixed_chan, "seq", split_axis=0, concat_axis=1, tiled=True),
        lax.all_to_all(grad_chan, "seq", split_axis=0, concat_axis=1, tiled=True),
    )
    output = (gate_second.astype(jnp.float32) * mixed_seq.astype(jnp.float32)).astype(jnp.bfloat16)
    next_input = from_behind(output, "pipe", 1)
    grad_decay = jnp.sum(grad_kernel * kernel * (-positions / length), axis=0)
    grad_raw = grad_kernel * envelope
    grad_filter_w = contract("ft,tc->fc", activation, grad_raw)
    grad_preact = contract("fc,tc->ft", filter_w, grad_raw) * jnp.cos(preact)
    part_weight = contract("et,ft->ef", features, grad_preact)
    part_bias = jnp.sum(grad_preact, axis=1)
    grad_embed_w, grad_embed_b = lax.psum((part_weight, part_bias), "seq")
    grad_values = (grad_weighted.astype(jnp.float32) * gate_first.astype(jnp.float32)).astype(
        jnp.bfloat16
    )
    grad_first = (grad_weighted.astype(jnp.float32) * values.astype(jnp.float32)).astype(
        jnp.bfloat16
    )
    grad_second = (cotangent.astype(jnp.float32) * mixed_seq.astype(jnp.float32)).astype(
        jnp.bfloat16
    )
    moved_values, moved_first, moved_second = from_behind(
        (grad_values, grad_first, grad_second), "pipe", -1
    )
    return (
        next_input[None],
        moved_values[None],
        moved_first[None],
        moved_second[None],
        grad_embed_w[None],
        grad_embed_b[None],
        grad_filter_w[None],
        grad_decay[None],
        grad_skip[None],
    )


def solution(mesh):
    return jax.shard_map(
        per_device,
        mesh=mesh,
        in_specs=(
            P("pipe", "seq", None),
            P("pipe", "seq", None),
            P("pipe", "seq", None),
            P("pipe", "seq", None),
            P("pipe", None, None),
            P("pipe", None),
            P("pipe", None, "seq"),
            P("pipe", "seq"),
            P("pipe", "seq"),
        ),
        out_specs=(
            P("pipe", "seq", None),
            P("pipe", "seq", None),
            P("pipe", "seq", None),
            P("pipe", "seq", None),
            P("pipe", None, None),
            P("pipe", None),
            P("pipe", None, "seq"),
            P("pipe", "seq"),
            P("pipe", "seq"),
        ),
        check_vma=False,
    )
```

```python
import functools
import math

import jax
import jax.numpy as jnp
import numpy as np
from jax import lax
from jax.experimental import pallas as pl
from jax.experimental.pallas import tpu as pltpu
from jax.sharding import PartitionSpec as P

E = 33


def from_behind(value, axis, steps):
    count = lax.axis_size(axis)
    pairs = [(source, (source + steps) % count) for source in range(count)]
    return lax.ppermute(value, axis, pairs)


def contract(form, left, right):
    return jnp.einsum(form, left, right, precision=lax.Precision.HIGHEST)


def position_features(length):
    position_ids = jnp.arange(length, dtype=jnp.int32)
    band_count = (E - 1) // 2
    band_index = jnp.arange(1, band_count + 1, dtype=jnp.int32)
    turn_ids = band_index[:, None] * band_index[:, None] * position_ids[None, :] % length
    angles = 2.0 * math.pi / length * turn_ids.astype(jnp.float32)
    position_ramp = position_ids.astype(jnp.float32)[None, :] / length
    return jnp.concatenate([position_ramp, jnp.cos(angles), jnp.sin(angles)], axis=0)


def build_tables(length):
    fft_total = 2 * length
    outer_len = 128
    half_len = outer_len // 2
    kept_len = half_len + 1
    inner_len = fft_total // outer_len
    index_kept = jnp.arange(kept_len, dtype=jnp.int32)
    index_half = jnp.arange(half_len, dtype=jnp.int32)
    index_inner = jnp.arange(inner_len, dtype=jnp.int32)
    angle_outer = (
        2.0
        * math.pi
        / outer_len
        * (index_kept[:, None] * index_half[None, :] % outer_len).astype(jnp.float32)
    )
    cos_outer = jnp.cos(angle_outer)
    sin_outer = jnp.sin(angle_outer)
    table_first = jnp.concatenate([cos_outer, -sin_outer], axis=0)
    angle_twist = (
        2.0
        * math.pi
        / fft_total
        * (index_kept[:, None] * index_inner[None, :] % fft_total).astype(jnp.float32)
    )
    cos_twist = jnp.cos(angle_twist)[:, :, None]
    sin_twist = jnp.sin(angle_twist)[:, :, None]
    angle_inner = (
        2.0
        * math.pi
        / inner_len
        * (index_inner[:, None] * index_inner[None, :] % inner_len).astype(jnp.float32)
    )
    cos_inner = jnp.cos(angle_inner)
    sin_inner = jnp.sin(angle_inner)
    table_second = jnp.stack(
        [jnp.stack([cos_inner, sin_inner], axis=1), jnp.stack([-sin_inner, cos_inner], axis=1)],
        axis=0,
    )
    table_back = jnp.stack(
        [jnp.stack([cos_inner, -sin_inner], axis=1), jnp.stack([sin_inner, cos_inner], axis=1)],
        axis=0,
    )
    weight_kept = (
        jnp.where((index_kept == 0) | (index_kept == half_len), 1.0, 2.0).astype(jnp.float32)
        / fft_total
    )
    table_last = jnp.stack(
        [
            jnp.transpose(cos_outer) * weight_kept[None, :],
            -jnp.transpose(sin_outer) * weight_kept[None, :],
        ],
        axis=1,
    )
    return (
        table_first,
        cos_twist,
        sin_twist,
        table_second,
        table_back,
        table_last,
        half_len,
        kept_len,
        inner_len,
    )


def staged_forward(field, tables_all):
    (
        table_first,
        cos_twist,
        sin_twist,
        table_second,
        table_back,
        table_last,
        half_len,
        kept_len,
        inner_len,
    ) = tables_all
    columns = field.shape[1]
    shaped = field.reshape(half_len, inner_len, columns)
    stacked = contract("kn,npc->kpc", table_first, shaped)
    part_re = stacked[:kept_len]
    part_im = stacked[kept_len:]
    twisted = jnp.stack(
        [part_re * cos_twist + part_im * sin_twist, part_im * cos_twist - part_re * sin_twist],
        axis=0,
    )
    return contract("sqrp,rkpc->skqc", table_second, twisted)


def staged_inverse(spec, tables_all):
    (
        table_first,
        cos_twist,
        sin_twist,
        table_second,
        table_back,
        table_last,
        half_len,
        kept_len,
        inner_len,
    ) = tables_all
    columns = spec.shape[3]
    sectioned = contract("sprq,rkqc->skpc", table_back, spec)
    section_re = sectioned[0]
    section_im = sectioned[1]
    twisted = jnp.stack(
        [
            section_re * cos_twist - section_im * sin_twist,
            section_im * cos_twist + section_re * sin_twist,
        ],
        axis=0,
    )
    result = contract("nrk,rkpc->npc", table_last, twisted)
    return result.reshape(half_len * inner_len, columns)


ROWS = 128
PAIR = 2 * ROWS
PADDED = 40


def split_tables(length):
    blocks = length // ROWS
    fine = np.arange(ROWS)
    coarse = np.arange(blocks) * ROWS
    point = np.arange(length)
    unit = math.pi / (2 * length)

    def pair(count, scale=1.0):
        angle = unit * (count % (4 * length))
        return [
            jnp.asarray((np.cos(angle) * scale).astype(np.float32)),
            jnp.asarray((np.sin(angle) * scale).astype(np.float32)),
        ]

    odd = 2 * point + 1
    ahead = pair((2 * fine + 1)[:, None] * point[None]) + pair((2 * coarse)[:, None] * point[None])
    back = pair(fine[:, None] * odd[None], 1.0 / length) + pair(coarse[:, None] * odd[None])
    return ahead + back


def padded_features(length):
    position = np.arange(length)
    band = np.arange(1, (E - 1) // 2 + 1)
    angle = 2.0 * math.pi / length * ((band[:, None] ** 2 * position[None]) % length)
    table = np.zeros((PADDED, length), np.float32)
    table[0] = position / length
    table[1 : 1 + len(band)] = np.cos(angle)
    table[1 + len(band) : E] = np.sin(angle)
    table[E] = 1.0
    return table


def section_kernel(
    shards, pipes,
    v_in, g1_in, g2_in, og_in, feat_in, feat_t_in,
    dc_in, ds_in, ec_in, es_in, bc_in, bs_in, ac_in, asn_in,
    wf, decay, skip, w_t, bias,
    o_next, o_val, o_first, o_second, o_emb, o_wf, o_decay, o_skip,
    ahead, back, kb, kf, env, kspec, wspec, prod, corr, graw,
    wsend, usend, wch, uch, mch, gch, mseq, gseq, stage, part, parts,
    v, g1, og, g2, feat_t, dc, ds, ec, es, bc, bs, ac, asn, feat, wext_t, loaded,
    a_send, a_recv, p_send, p_recv, x_send, x_recv,
):
    f32, bf16 = jnp.float32, jnp.bfloat16
    length = shards * ROWS
    width = wf.shape[1]
    pipe = lax.axis_index("pipe")
    me = lax.axis_index("seq")
    mine = me // 2
    partner = me + 1 - 2 * (me % 2)
    pairs = shards // 2
    nxt = (pipe + 1) % pipes
    prv = (pipe + pipes - 1) % pipes
    high = lax.Precision.HIGHEST

    def peer(step, sign):
        far = 1 + step // 2
        return ((mine + sign * far + pairs) % pairs) * 2 + step % 2

    def others(sign, visit):
        def body(step, carry):
            visit(peer(step, sign))
            return carry

        lax.fori_loop(0, shards - 2, body, 0)
        visit(partner)

    def rows(index):
        return pl.ds(pl.multiple_of(index * ROWS, ROWS), ROWS)

    def cols(index):
        return pl.ds(pl.multiple_of(index * width, width), width)

    def wide(index):
        return pl.ds(pl.multiple_of(index * PAIR, PAIR), PAIR)

    def exchange(kind, src, dst, there, source):
        return pltpu.make_async_remote_copy(
            src_ref=src, dst_ref=dst, send_sem=a_send.at[kind, there],
            recv_sem=a_recv.at[kind, source], device_id=(pipe, there),
            device_id_type=pl.DeviceIdType.MESH,
        )

    def handed(kind, slot):
        out = (o_next, o_second, o_val, o_first)[kind]
        return pltpu.make_async_remote_copy(
            src_ref=stage.at[kind, slot], dst_ref=out.at[:, cols(slot)],
            send_sem=p_send.at[kind, slot], recv_sem=p_recv.at[kind, slot],
            device_id=(nxt if kind == 0 else prv, me),
            device_id_type=pl.DeviceIdType.MESH,
        )

    def shared(there, source):
        return pltpu.make_async_remote_copy(
            src_ref=part, dst_ref=parts.at[source], send_sem=x_send.at[there],
            recv_sem=x_recv.at[source], device_id=(pipe, there),
            device_id_type=pl.DeviceIdType.MESH,
        )

    def times(one, two, index):
        return (one[:, cols(index)].astype(f32) * two[:, cols(index)].astype(f32)).astype(bf16)

    loads = [
        pltpu.make_async_copy(src, dst, loaded.at[index])
        for index, (src, dst) in enumerate((
            (v_in, v), (g1_in, g1), (feat_t_in, feat_t), (dc_in, dc), (ds_in, ds), (ec_in, ec),
            (es_in, es), (og_in, og), (g2_in, g2), (bc_in, bc), (bs_in, bs), (ac_in, ac),
            (asn_in, asn), (feat_in, feat),
        ))
    ]
    for load in loads:
        load.start()
    barrier = pltpu.get_barrier_semaphore()

    def greet(there):
        pl.semaphore_signal(
            barrier, inc=1, device_id=(pipe, there), device_id_type=pl.DeviceIdType.MESH
        )

    others(1, greet)
    for side in (nxt, prv):
        pl.semaphore_signal(
            barrier, inc=1, device_id=(side, me), device_id_type=pl.DeviceIdType.MESH
        )
    hidden = wf.shape[0]
    lane = lax.broadcasted_iota(jnp.int32, (hidden, hidden), 1)
    line = lax.broadcasted_iota(jnp.int32, (hidden, hidden), 0)
    column = jnp.sum(jnp.where(lane == line, bias[...], 0.0), axis=1, keepdims=True)
    wext_t[...] = jnp.zeros_like(wext_t)
    wext_t[:, :E] = w_t[...]
    wext_t[:, E : E + 1] = column
    for load in loads[:2]:
        load.wait()
    pl.semaphore_wait(barrier, shards + 1)

    def send_weighted(there):
        wsend[there] = times(v, g1, there)
        exchange(0, wsend.at[there], wch.at[rows(me), :], there, me).start()

    others(1, send_weighted)
    wch[rows(me), :] = times(v, g1, me)

    for load in loads[2:7]:
        load.wait()

    def make_kernel(tile, carry):
        here = wide(tile)
        step = (lax.broadcasted_iota(jnp.int32, (PAIR, 1), 0) + tile * PAIR).astype(f32)
        act = jnp.sin(lax.dot_general(
            feat_t[here, :], wext_t[...], (((1,), (1,)), ((), ())), precision=high
        ))
        envelope = jnp.exp(-decay[...] * step / length) * (1.0 / math.sqrt(length))
        kernel = jnp.dot(act, wf[...], precision=high) * envelope
        env[here, :] = envelope
        kf[here, :] = kernel
        kb[here, :] = kernel.astype(bf16)
        return carry

    lax.fori_loop(0, length // PAIR, make_kernel, 0)

    def make_ahead(tile, carry):
        row_c, row_s = ec[pl.ds(tile, 1), :], es[pl.ds(tile, 1), :]
        base = pl.multiple_of(tile * PAIR, PAIR)
        ahead[pl.ds(base, ROWS), :] = (dc[...] * row_c - ds[...] * row_s).astype(bf16)
        ahead[pl.ds(base + ROWS, ROWS), :] = (-(ds[...] * row_c + dc[...] * row_s)).astype(bf16)
        return carry

    lax.fori_loop(0, shards, make_ahead, 0)

    def make_kspec(tile, carry):
        kspec[wide(tile), :] = jnp.dot(
            ahead[wide(tile), :], kb[...], preferred_element_type=f32
        )
        return carry

    lax.fori_loop(0, shards, make_kspec, 0)

    for load in loads[7:]:
        load.wait()

    def send_upstream(there):
        usend[there] = times(og, g2, there)
        exchange(1, usend.at[there], uch.at[rows(me), :], there, me).start()

    others(1, send_upstream)
    uch[rows(me), :] = times(og, g2, me)

    def make_back(tile, carry):
        full_c, full_s = ac[pl.ds(tile, 1), :], asn[pl.ds(tile, 1), :]
        for block in range(shards):
            lanes = slice(block * ROWS, (block + 1) * ROWS)
            row_c, row_s = full_c[:, lanes], full_s[:, lanes]
            cos_b, sin_b = bc[:, lanes], bs[:, lanes]
            start = block * PAIR
            back[rows(tile), start : start + ROWS] = (cos_b * row_c - sin_b * row_s).astype(bf16)
            back[rows(tile), start + ROWS : start + PAIR] = (
                -(sin_b * row_c + cos_b * row_s)
            ).astype(bf16)
        return carry

    lax.fori_loop(0, shards, make_back, 0)

    others(-1, lambda source: exchange(
        0, wsend.at[source], wch.at[rows(source), :], source, source).wait_recv())

    def make_product(tile, carry):
        here = wide(tile)
        spec = jnp.dot(ahead[here, :], wch[...], preferred_element_type=f32)
        wspec[here, :] = spec
        k_re, k_im = kspec[here, :][:ROWS], kspec[here, :][ROWS:]
        x_re, x_im = spec[:ROWS], spec[ROWS:]
        prod[here, :] = jnp.concatenate(
            [k_re * x_re - k_im * x_im, k_re * x_im + k_im * x_re], axis=0
        ).astype(bf16)
        return carry

    lax.fori_loop(0, shards, make_product, 0)

    def convolved(kind, field, result, landing):
        def chunk(index):
            here = wide(index)
            conv = jnp.dot(back[here, :], prod[...], preferred_element_type=f32)
            result[here, :] = (conv + skip[...] * field[here, :].astype(f32)).astype(bf16)

        def far(step, carry):
            index = (mine + 1 + step) % pairs
            chunk(index)
            for side in range(2):
                there = index * 2 + side
                exchange(kind, result.at[rows(there), :], landing.at[me], there, me).start()
            return carry

        lax.fori_loop(0, pairs - 1, far, 0)
        chunk(mine)
        exchange(kind, result.at[rows(partner), :], landing.at[me], partner, me).start()
        landing[me] = result[rows(me), :]

    convolved(2, wch, mch, mseq)

    others(-1, lambda source: exchange(
        1, usend.at[source], uch.at[rows(source), :], source, source).wait_recv())

    def make_products(tile, carry):
        here = wide(tile)
        spec = jnp.dot(ahead[here, :], uch[...], preferred_element_type=f32)
        x_re, x_im = spec[:ROWS], spec[ROWS:]
        for left, target in ((kspec, prod), (wspec, corr)):
            l_re, l_im = left[here, :][:ROWS], left[here, :][ROWS:]
            target[here, :] = jnp.concatenate(
                [l_re * x_re + l_im * x_im, l_re * x_im - l_im * x_re], axis=0
            ).astype(bf16)
        return carry

    lax.fori_loop(0, shards, make_products, 0)
    convolved(3, uch, gch, gseq)

    def pass_mixed(source):
        block = mseq[source].astype(f32)
        stage[0, source] = (g2[:, cols(source)].astype(f32) * block).astype(bf16)
        stage[1, source] = (og[:, cols(source)].astype(f32) * block).astype(bf16)
        handed(0, source).start()
        handed(1, source).start()

    def land_mixed(source):
        exchange(2, mch.at[rows(source), :], mseq.at[source], source, source).wait_recv()
        pass_mixed(source)

    pass_mixed(me)
    others(-1, land_mixed)

    def correlate(tile, carry):
        here = wide(tile)
        step = (lax.broadcasted_iota(jnp.int32, (PAIR, 1), 0) + tile * PAIR).astype(f32)
        grad = jnp.dot(back[here, :], corr[...], preferred_element_type=f32)
        graw[here, :] = (grad * env[here, :]).astype(bf16)
        sum_d, sum_s = carry
        sum_d += jnp.sum(grad * kf[here, :] * (-step / length), axis=0, keepdims=True)
        both = uch[here, :].astype(f32) * wch[here, :].astype(f32)
        return sum_d, sum_s + jnp.sum(both, axis=0, keepdims=True)

    empty = jnp.zeros((1, width), f32)
    sum_d, sum_s = lax.fori_loop(0, length // PAIR, correlate, (empty, empty))
    o_decay[...] = sum_d
    o_skip[...] = sum_s

    def halves(value):
        top = value.astype(bf16)
        return jnp.concatenate([top, (value - top.astype(f32)).astype(bf16)], axis=0)

    preact = jnp.dot(wext_t[...], feat[...], precision=high)
    both = jnp.dot(halves(jnp.sin(preact)), graw[...], preferred_element_type=f32)
    o_wf[...] = both[:hidden] + both[hidden:]
    both = lax.dot_general(
        halves(wf[...]), graw[...], (((1,), (1,)), ((), ())), preferred_element_type=f32
    )
    grad_pre = (both[:hidden] + both[hidden:]) * jnp.cos(preact)
    part[...] = lax.dot_general(
        feat[...], jnp.concatenate([grad_pre, jnp.zeros_like(grad_pre)], axis=0),
        (((1,), (1,)), ((), ())), precision=high,
    )
    others(1, lambda there: shared(there, me).start())

    def pass_grad(source):
        block = gseq[source].astype(f32)
        stage[2, source] = (g1[:, cols(source)].astype(f32) * block).astype(bf16)
        stage[3, source] = (v[:, cols(source)].astype(f32) * block).astype(bf16)
        handed(2, source).start()
        handed(3, source).start()

    def land_grad(source):
        exchange(3, gch.at[rows(source), :], gseq.at[source], source, source).wait_recv()
        pass_grad(source)

    pass_grad(me)
    others(-1, land_grad)

    parts[me] = part[...]
    others(-1, lambda source: shared(source, source).wait_recv())
    total = parts[0]
    for index in range(1, shards):
        total = total + parts[index]
    o_emb[...] = total

    def sent(there):
        exchange(0, wsend.at[there], wch.at[rows(me), :], there, me).wait_send()
        exchange(1, usend.at[there], uch.at[rows(me), :], there, me).wait_send()
        exchange(2, mch.at[rows(there), :], mseq.at[me], there, me).wait_send()
        exchange(3, gch.at[rows(there), :], gseq.at[me], there, me).wait_send()
        shared(there, me).wait_send()

    others(1, sent)

    def finish(slot, carry):
        for kind in range(4):
            handed(kind, slot).wait()
        return carry

    lax.fori_loop(0, shards, finish, 0)


CHUNKS = 4


def finish_kernel(
    a_in, b_in, c_in, d_in, emb, wf, row_d, row_s,
    a_out, b_out, c_out, d_out, o_emb, o_bias, o_wf, o_d, o_s, held, got, put,
):
    rows = ROWS // CHUNKS
    reads, writes = [], []
    for kind, (src, dst) in enumerate(
        ((a_in, a_out), (b_in, b_out), (c_in, c_out), (d_in, d_out))
    ):
        for chunk in range(CHUNKS):
            here = pl.ds(chunk * rows, rows)
            index = kind * CHUNKS + chunk
            middle = held.at[kind, here, :]
            reads.append(pltpu.make_async_copy(src.at[here, :], middle, got.at[index]))
            writes.append(pltpu.make_async_copy(middle, dst.at[0, here, :], put.at[index]))
    for read in reads:
        read.start()
    o_emb[0] = emb[:E, : o_emb.shape[2]]
    o_bias[...] = emb[E : E + 1, : o_bias.shape[1]]
    o_wf[0] = wf[...]
    o_d[...] = row_d[...]
    o_s[...] = row_s[...]
    for read, write in zip(reads, writes):
        read.wait()
        write.start()
    for write in writes:
        write.wait()


def fused_section(v, g1, g2, og, w_embed, b_embed, wf, decay, skip):
    shards = lax.axis_size("seq")
    pipes = lax.axis_size("pipe")
    length = shards * ROWS
    wide_cols = v.shape[1]
    width = wf.shape[1]
    hidden = wf.shape[0]
    f32, bf16 = jnp.float32, jnp.bfloat16
    feat = padded_features(length)
    tables = split_tables(length)
    vmem = pl.BlockSpec(memory_space=pltpu.VMEM)
    hbm = pl.BlockSpec(memory_space=pl.ANY)
    stream = jax.ShapeDtypeStruct((ROWS, wide_cols), bf16)
    row = jax.ShapeDtypeStruct((1, width), f32)
    dma = pltpu.SemaphoreType.DMA
    results = pl.pallas_call(
        functools.partial(section_kernel, shards, pipes),
        out_shape=(
            stream, stream, stream, stream,
            jax.ShapeDtypeStruct((PADDED, 2 * hidden), f32),
            jax.ShapeDtypeStruct((hidden, width), f32), row, row,
        ),
        in_specs=[hbm] * 14 + [vmem] * 5,
        out_specs=(hbm,) * 4 + (vmem,) * 4,
        scratch_shapes=[
            pltpu.VMEM((2 * length, length), bf16),
            pltpu.VMEM((length, 2 * length), bf16),
            pltpu.VMEM((length, width), bf16),
            pltpu.VMEM((length, width), f32),
            pltpu.VMEM((length, width), f32),
            pltpu.VMEM((2 * length, width), f32),
            pltpu.VMEM((2 * length, width), f32),
            pltpu.VMEM((2 * length, width), bf16),
            pltpu.VMEM((2 * length, width), bf16),
            pltpu.VMEM((length, width), bf16),
            pltpu.VMEM((shards, ROWS, width), bf16),
            pltpu.VMEM((shards, ROWS, width), bf16),
            pltpu.VMEM((length, width), bf16),
            pltpu.VMEM((length, width), bf16),
            pltpu.VMEM((length, width), bf16),
            pltpu.VMEM((length, width), bf16),
            pltpu.VMEM((shards, ROWS, width), bf16),
            pltpu.VMEM((shards, ROWS, width), bf16),
            pltpu.VMEM((4, shards, ROWS, width), bf16),
            pltpu.VMEM((PADDED, 2 * hidden), f32),
            pltpu.VMEM((shards, PADDED, 2 * hidden), f32),
            *[pltpu.VMEM((ROWS, wide_cols), bf16)] * 4,
            pltpu.VMEM((length, PADDED), f32),
            *[pltpu.VMEM((ROWS, length), f32)] * 2,
            *[pltpu.VMEM((shards, length), f32)] * 2,
            *[pltpu.VMEM((ROWS, length), f32)] * 2,
            *[pltpu.VMEM((shards, length), f32)] * 2,
            pltpu.VMEM((PADDED, length), f32),
            pltpu.VMEM((hidden, PADDED), f32),
            dma((14,)),
            dma((4, shards)), dma((4, shards)),
            dma((4, shards)), dma((4, shards)),
            dma((shards,)), dma((shards,)),
        ],
        compiler_params=pltpu.CompilerParams(
            collective_id=0, has_side_effects=True, vmem_limit_bytes=60 * 1024 * 1024
        ),
    )(
        v, g1, g2, og, jnp.asarray(feat), jnp.asarray(feat.T.copy()), *tables,
        wf, decay[None], skip[None], w_embed.T, b_embed[None],
    )
    final = jax.ShapeDtypeStruct((1, ROWS, wide_cols), bf16)
    return tuple(
        pl.pallas_call(
            finish_kernel,
            out_shape=(
                final, final, final, final,
                jax.ShapeDtypeStruct((1, E, hidden), f32),
                jax.ShapeDtypeStruct((1, hidden), f32),
                jax.ShapeDtypeStruct((1, hidden, width), f32), row, row,
            ),
            in_specs=[hbm] * 4 + [vmem] * 4,
            out_specs=(hbm,) * 4 + (vmem,) * 5,
            scratch_shapes=[
                pltpu.VMEM((4, ROWS, wide_cols), bf16),
                dma((4 * CHUNKS,)), dma((4 * CHUNKS,)),
            ],
            compiler_params=pltpu.CompilerParams(vmem_limit_bytes=60 * 1024 * 1024),
        )(*results)
    )


def spectral_product(left, right, conjugate_left):
    left_re = left[0]
    left_im = left[1]
    right_re = right[0]
    right_im = right[1]
    if conjugate_left:
        left_im = -left_im
    return jnp.stack(
        [left_re * right_re - left_im * right_im, left_re * right_im + left_im * right_re], axis=0
    )


def per_device(value_in, gate_one, gate_two, out_grad, w_embed, b_embed, w_filter, decay, skip):
    values = value_in[0]
    gate_first = gate_one[0]
    gate_second = gate_two[0]
    cotangent = out_grad[0]
    filter_w = w_filter[0]
    shards = lax.axis_size("seq")
    length = values.shape[0] * shards
    if length <= 1024 and values.shape[0] == ROWS and shards % 2 == 0 and lax.axis_size("pipe") > 2:
        return fused_section(
            values, gate_first, gate_second, cotangent,
            w_embed[0], b_embed[0], filter_w, decay[0], skip[0],
        )
    weighted = (values.astype(jnp.float32) * gate_first.astype(jnp.float32)).astype(jnp.bfloat16)
    upstream = (cotangent.astype(jnp.float32) * gate_second.astype(jnp.float32)).astype(
        jnp.bfloat16
    )
    features = position_features(length)
    preact = contract("ef,et->ft", w_embed[0], features) + b_embed[0][:, None]
    activation = jnp.sin(preact)
    positions = jnp.arange(length, dtype=jnp.int32).astype(jnp.float32)[:, None]
    envelope = jnp.exp(-decay[0][None, :] * positions / length) * (1.0 / math.sqrt(length))
    kernel = contract("ft,fc->tc", activation, filter_w) * envelope
    tables_all = build_tables(length)
    forward_transform, inverse_transform = staged_forward, staged_inverse
    kernel_spec = forward_transform(kernel, tables_all)
    skip_row = skip[0][None, :]
    weighted_chan, upstream_chan = (
        lax.all_to_all(weighted, "seq", split_axis=1, concat_axis=0, tiled=True),
        lax.all_to_all(upstream, "seq", split_axis=1, concat_axis=0, tiled=True),
    )
    weighted_f = weighted_chan.astype(jnp.float32)
    weighted_spec = forward_transform(weighted_f, tables_all)
    conv = inverse_transform(spectral_product(kernel_spec, weighted_spec, False), tables_all)
    mixed_chan, weighted_f, weighted_spec = (
        (conv + skip_row * weighted_f).astype(jnp.bfloat16),
        weighted_f,
        weighted_spec,
    )
    upstream_f = upstream_chan.astype(jnp.float32)
    upstream_spec = forward_transform(upstream_f, tables_all)
    backward_conv = inverse_transform(
        spectral_product(kernel_spec, upstream_spec, True), tables_all
    )
    grad_chan = (backward_conv + skip_row * upstream_f).astype(jnp.bfloat16)
    grad_skip = jnp.sum(upstream_f * weighted_f, axis=0)
    grad_kernel = inverse_transform(
        spectral_product(weighted_spec, upstream_spec, True), tables_all
    )
    grad_chan, grad_skip, grad_kernel = (grad_chan, grad_skip, grad_kernel)
    mixed_seq, grad_weighted = (
        lax.all_to_all(mixed_chan, "seq", split_axis=0, concat_axis=1, tiled=True),
        lax.all_to_all(grad_chan, "seq", split_axis=0, concat_axis=1, tiled=True),
    )
    output = (gate_second.astype(jnp.float32) * mixed_seq.astype(jnp.float32)).astype(jnp.bfloat16)
    next_input = from_behind(output, "pipe", 1)
    grad_decay = jnp.sum(grad_kernel * kernel * (-positions / length), axis=0)
    grad_raw = grad_kernel * envelope
    grad_filter_w = contract("ft,tc->fc", activation, grad_raw)
    grad_preact = contract("fc,tc->ft", filter_w, grad_raw) * jnp.cos(preact)
    part_weight = contract("et,ft->ef", features, grad_preact)
    part_bias = jnp.sum(grad_preact, axis=1)
    grad_embed_w, grad_embed_b = lax.psum((part_weight, part_bias), "seq")
    grad_values = (grad_weighted.astype(jnp.float32) * gate_first.astype(jnp.float32)).astype(
        jnp.bfloat16
    )
    grad_first = (grad_weighted.astype(jnp.float32) * values.astype(jnp.float32)).astype(
        jnp.bfloat16
    )
    grad_second = (cotangent.astype(jnp.float32) * mixed_seq.astype(jnp.float32)).astype(
        jnp.bfloat16
    )
    moved_values, moved_first, moved_second = from_behind(
        (grad_values, grad_first, grad_second), "pipe", -1
    )
    return (
        next_input[None],
        moved_values[None],
        moved_first[None],
        moved_second[None],
        grad_embed_w[None],
        grad_embed_b[None],
        grad_filter_w[None],
        grad_decay[None],
        grad_skip[None],
    )


def solution(mesh):
    return jax.shard_map(
        per_device,
        mesh=mesh,
        in_specs=(
            P("pipe", "seq", None),
            P("pipe", "seq", None),
            P("pipe", "seq", None),
            P("pipe", "seq", None),
            P("pipe", None, None),
            P("pipe", None),
            P("pipe", None, "seq"),
            P("pipe", "seq"),
            P("pipe", "seq"),
        ),
        out_specs=(
            P("pipe", "seq", None),
            P("pipe", "seq", None),
            P("pipe", "seq", None),
            P("pipe", "seq", None),
            P("pipe", None, None),
            P("pipe", None),
            P("pipe", None, "seq"),
            P("pipe", "seq"),
            P("pipe", "seq"),
        ),
        check_vma=False,
    )
```

```python
import functools
import math

import jax
import jax.numpy as jnp
import numpy as np
from jax import lax
from jax.experimental import pallas as pl
from jax.experimental.pallas import tpu as pltpu
from jax.sharding import PartitionSpec as P

E = 33


def from_behind(value, axis, steps):
    count = lax.axis_size(axis)
    pairs = [(source, (source + steps) % count) for source in range(count)]
    return lax.ppermute(value, axis, pairs)


def contract(form, left, right):
    return jnp.einsum(form, left, right, precision=lax.Precision.HIGHEST)


def position_features(length):
    position_ids = jnp.arange(length, dtype=jnp.int32)
    band_count = (E - 1) // 2
    band_index = jnp.arange(1, band_count + 1, dtype=jnp.int32)
    turn_ids = band_index[:, None] * band_index[:, None] * position_ids[None, :] % length
    angles = 2.0 * math.pi / length * turn_ids.astype(jnp.float32)
    position_ramp = position_ids.astype(jnp.float32)[None, :] / length
    return jnp.concatenate([position_ramp, jnp.cos(angles), jnp.sin(angles)], axis=0)


def build_tables(length):
    fft_total = 2 * length
    outer_len = 128
    half_len = outer_len // 2
    kept_len = half_len + 1
    inner_len = fft_total // outer_len
    index_kept = jnp.arange(kept_len, dtype=jnp.int32)
    index_half = jnp.arange(half_len, dtype=jnp.int32)
    index_inner = jnp.arange(inner_len, dtype=jnp.int32)
    angle_outer = (
        2.0
        * math.pi
        / outer_len
        * (index_kept[:, None] * index_half[None, :] % outer_len).astype(jnp.float32)
    )
    cos_outer = jnp.cos(angle_outer)
    sin_outer = jnp.sin(angle_outer)
    table_first = jnp.concatenate([cos_outer, -sin_outer], axis=0)
    angle_twist = (
        2.0
        * math.pi
        / fft_total
        * (index_kept[:, None] * index_inner[None, :] % fft_total).astype(jnp.float32)
    )
    cos_twist = jnp.cos(angle_twist)[:, :, None]
    sin_twist = jnp.sin(angle_twist)[:, :, None]
    angle_inner = (
        2.0
        * math.pi
        / inner_len
        * (index_inner[:, None] * index_inner[None, :] % inner_len).astype(jnp.float32)
    )
    cos_inner = jnp.cos(angle_inner)
    sin_inner = jnp.sin(angle_inner)
    table_second = jnp.stack(
        [jnp.stack([cos_inner, sin_inner], axis=1), jnp.stack([-sin_inner, cos_inner], axis=1)],
        axis=0,
    )
    table_back = jnp.stack(
        [jnp.stack([cos_inner, -sin_inner], axis=1), jnp.stack([sin_inner, cos_inner], axis=1)],
        axis=0,
    )
    weight_kept = (
        jnp.where((index_kept == 0) | (index_kept == half_len), 1.0, 2.0).astype(jnp.float32)
        / fft_total
    )
    table_last = jnp.stack(
        [
            jnp.transpose(cos_outer) * weight_kept[None, :],
            -jnp.transpose(sin_outer) * weight_kept[None, :],
        ],
        axis=1,
    )
    return (
        table_first,
        cos_twist,
        sin_twist,
        table_second,
        table_back,
        table_last,
        half_len,
        kept_len,
        inner_len,
    )


def staged_forward(field, tables_all):
    (
        table_first,
        cos_twist,
        sin_twist,
        table_second,
        table_back,
        table_last,
        half_len,
        kept_len,
        inner_len,
    ) = tables_all
    columns = field.shape[1]
    shaped = field.reshape(half_len, inner_len, columns)
    stacked = contract("kn,npc->kpc", table_first, shaped)
    part_re = stacked[:kept_len]
    part_im = stacked[kept_len:]
    twisted = jnp.stack(
        [part_re * cos_twist + part_im * sin_twist, part_im * cos_twist - part_re * sin_twist],
        axis=0,
    )
    return contract("sqrp,rkpc->skqc", table_second, twisted)


def staged_inverse(spec, tables_all):
    (
        table_first,
        cos_twist,
        sin_twist,
        table_second,
        table_back,
        table_last,
        half_len,
        kept_len,
        inner_len,
    ) = tables_all
    columns = spec.shape[3]
    sectioned = contract("sprq,rkqc->skpc", table_back, spec)
    section_re = sectioned[0]
    section_im = sectioned[1]
    twisted = jnp.stack(
        [
            section_re * cos_twist - section_im * sin_twist,
            section_im * cos_twist + section_re * sin_twist,
        ],
        axis=0,
    )
    result = contract("nrk,rkpc->npc", table_last, twisted)
    return result.reshape(half_len * inner_len, columns)


ROWS = 128
PAIR = 2 * ROWS
PADDED = 40


def split_tables(length):
    blocks = length // ROWS
    fine = np.arange(ROWS)
    coarse = np.arange(blocks) * ROWS
    point = np.arange(length)
    unit = math.pi / (2 * length)

    def pair(count, scale=1.0):
        angle = unit * (count % (4 * length))
        return [
            jnp.asarray((np.cos(angle) * scale).astype(np.float32)),
            jnp.asarray((np.sin(angle) * scale).astype(np.float32)),
        ]

    odd = 2 * point + 1
    ahead = pair((2 * fine + 1)[:, None] * point[None]) + pair((2 * coarse)[:, None] * point[None])
    back = pair(fine[:, None] * odd[None], 1.0 / length) + pair(coarse[:, None] * odd[None])
    return ahead + back


def padded_features(length):
    position = np.arange(length)
    band = np.arange(1, (E - 1) // 2 + 1)
    angle = 2.0 * math.pi / length * ((band[:, None] ** 2 * position[None]) % length)
    table = np.zeros((PADDED, length), np.float32)
    table[0] = position / length
    table[1 : 1 + len(band)] = np.cos(angle)
    table[1 + len(band) : E] = np.sin(angle)
    table[E] = 1.0
    return table


def section_kernel(
    shards, pipes,
    v_in, g1_in, g2_in, og_in, feat_in, feat_t_in,
    dc_in, ds_in, ec_in, es_in, bc_in, bs_in, ac_in, asn_in,
    wf, decay, skip, w_t, bias,
    o_next, o_val, o_first, o_second, o_emb, o_wf, o_decay, o_skip,
    ahead, back, kb, kf, env, kspec, wspec, prod, corr, graw,
    wsend, usend, wch, uch, mch, gch, mseq, gseq, stage, part, parts,
    v, g1, og, g2, feat_t, dc, ds, ec, es, bc, bs, ac, asn, feat, wext_t, loaded,
    a_send, a_recv, p_send, p_recv, x_send, x_recv,
):
    f32, bf16 = jnp.float32, jnp.bfloat16
    length = shards * ROWS
    width = wf.shape[1]
    pipe = lax.axis_index("pipe")
    me = lax.axis_index("seq")
    mine = me // 2
    partner = me + 1 - 2 * (me % 2)
    pairs = shards // 2
    nxt = (pipe + 1) % pipes
    prv = (pipe + pipes - 1) % pipes
    high = lax.Precision.HIGHEST

    def peer(step, sign):
        far = 1 + step // 2
        return ((mine + sign * far + pairs) % pairs) * 2 + step % 2

    def others(sign, visit):
        def body(step, carry):
            visit(peer(step, sign))
            return carry

        lax.fori_loop(0, shards - 2, body, 0)
        visit(partner)

    def rows(index):
        return pl.ds(pl.multiple_of(index * ROWS, ROWS), ROWS)

    def cols(index):
        return pl.ds(pl.multiple_of(index * width, width), width)

    def wide(index):
        return pl.ds(pl.multiple_of(index * PAIR, PAIR), PAIR)

    def exchange(kind, src, dst, there, source):
        return pltpu.make_async_remote_copy(
            src_ref=src, dst_ref=dst, send_sem=a_send.at[kind, there],
            recv_sem=a_recv.at[kind, source], device_id=(pipe, there),
            device_id_type=pl.DeviceIdType.MESH,
        )

    def handed(kind, slot):
        out = (o_next, o_second, o_val, o_first)[kind]
        return pltpu.make_async_remote_copy(
            src_ref=stage.at[kind, slot], dst_ref=out.at[:, cols(slot)],
            send_sem=p_send.at[kind, slot], recv_sem=p_recv.at[kind, slot],
            device_id=(nxt if kind == 0 else prv, me),
            device_id_type=pl.DeviceIdType.MESH,
        )

    def shared(there, source):
        return pltpu.make_async_remote_copy(
            src_ref=part, dst_ref=parts.at[source], send_sem=x_send.at[there],
            recv_sem=x_recv.at[source], device_id=(pipe, there),
            device_id_type=pl.DeviceIdType.MESH,
        )

    def times(one, two, index):
        return (one[:, cols(index)].astype(f32) * two[:, cols(index)].astype(f32)).astype(bf16)

    loads = [
        pltpu.make_async_copy(src, dst, loaded.at[index])
        for index, (src, dst) in enumerate((
            (v_in, v), (g1_in, g1), (feat_t_in, feat_t), (dc_in, dc), (ds_in, ds), (ec_in, ec),
            (es_in, es), (og_in, og), (g2_in, g2), (bc_in, bc), (bs_in, bs), (ac_in, ac),
            (asn_in, asn), (feat_in, feat),
        ))
    ]
    for load in loads:
        load.start()
    barrier = pltpu.get_barrier_semaphore()

    def greet(there):
        pl.semaphore_signal(
            barrier, inc=1, device_id=(pipe, there), device_id_type=pl.DeviceIdType.MESH
        )

    others(1, greet)
    for side in (nxt, prv):
        pl.semaphore_signal(
            barrier, inc=1, device_id=(side, me), device_id_type=pl.DeviceIdType.MESH
        )
    hidden = wf.shape[0]
    lane = lax.broadcasted_iota(jnp.int32, (hidden, hidden), 1)
    line = lax.broadcasted_iota(jnp.int32, (hidden, hidden), 0)
    column = jnp.sum(jnp.where(lane == line, bias[...], 0.0), axis=1, keepdims=True)
    wext_t[...] = jnp.zeros_like(wext_t)
    wext_t[:, :E] = w_t[...]
    wext_t[:, E : E + 1] = column
    for load in loads[:2]:
        load.wait()
    pl.semaphore_wait(barrier, shards + 1)

    def send_weighted(there):
        wsend[there] = times(v, g1, there)
        exchange(0, wsend.at[there], wch.at[rows(me), :], there, me).start()

    others(1, send_weighted)
    wch[rows(me), :] = times(v, g1, me)

    for load in loads[2:7]:
        load.wait()

    def make_kernel(tile, carry):
        here = wide(tile)
        step = (lax.broadcasted_iota(jnp.int32, (PAIR, 1), 0) + tile * PAIR).astype(f32)
        act = jnp.sin(lax.dot_general(
            feat_t[here, :], wext_t[...], (((1,), (1,)), ((), ())), precision=high
        ))
        envelope = jnp.exp(-decay[...] * step / length) * (1.0 / math.sqrt(length))
        kernel = jnp.dot(act, wf[...], precision=high) * envelope
        env[here, :] = envelope
        kf[here, :] = kernel
        kb[here, :] = kernel.astype(bf16)
        return carry

    lax.fori_loop(0, length // PAIR, make_kernel, 0)

    def make_ahead(tile, carry):
        row_c, row_s = ec[pl.ds(tile, 1), :], es[pl.ds(tile, 1), :]
        base = pl.multiple_of(tile * PAIR, PAIR)
        ahead[pl.ds(base, ROWS), :] = (dc[...] * row_c - ds[...] * row_s).astype(bf16)
        ahead[pl.ds(base + ROWS, ROWS), :] = (-(ds[...] * row_c + dc[...] * row_s)).astype(bf16)
        return carry

    lax.fori_loop(0, shards, make_ahead, 0)

    def make_kspec(tile, carry):
        kspec[wide(tile), :] = jnp.dot(
            ahead[wide(tile), :], kb[...], preferred_element_type=f32
        )
        return carry

    lax.fori_loop(0, shards, make_kspec, 0)

    for load in loads[7:]:
        load.wait()

    def make_back(tile, carry):
        full_c, full_s = ac[pl.ds(tile, 1), :], asn[pl.ds(tile, 1), :]
        for block in range(shards):
            lanes = slice(block * ROWS, (block + 1) * ROWS)
            row_c, row_s = full_c[:, lanes], full_s[:, lanes]
            cos_b, sin_b = bc[:, lanes], bs[:, lanes]
            start = block * PAIR
            back[rows(tile), start : start + ROWS] = (cos_b * row_c - sin_b * row_s).astype(bf16)
            back[rows(tile), start + ROWS : start + PAIR] = (
                -(sin_b * row_c + cos_b * row_s)
            ).astype(bf16)
        return carry

    lax.fori_loop(0, shards, make_back, 0)

    def send_upstream(there):
        usend[there] = times(og, g2, there)
        exchange(0, wsend.at[there], wch.at[rows(me), :], there, me).wait_send()
        exchange(1, usend.at[there], uch.at[rows(me), :], there, me).start()

    others(1, send_upstream)
    uch[rows(me), :] = times(og, g2, me)

    others(-1, lambda source: exchange(
        0, wsend.at[source], wch.at[rows(source), :], source, source).wait_recv())

    def make_product(tile, carry):
        here = wide(tile)
        spec = jnp.dot(ahead[here, :], wch[...], preferred_element_type=f32)
        wspec[here, :] = spec
        k_re, k_im = kspec[here, :][:ROWS], kspec[here, :][ROWS:]
        x_re, x_im = spec[:ROWS], spec[ROWS:]
        prod[here, :] = jnp.concatenate(
            [k_re * x_re - k_im * x_im, k_re * x_im + k_im * x_re], axis=0
        ).astype(bf16)
        return carry

    lax.fori_loop(0, shards, make_product, 0)

    def convolved(kind, field, result, landing):
        def chunk(index):
            here = wide(index)
            conv = jnp.dot(back[here, :], prod[...], preferred_element_type=f32)
            result[here, :] = (conv + skip[...] * field[here, :].astype(f32)).astype(bf16)

        def far(step, carry):
            index = (mine + 1 + step) % pairs
            chunk(index)
            for side in range(2):
                there = index * 2 + side
                exchange(kind, result.at[rows(there), :], landing.at[me], there, me).start()
            return carry

        lax.fori_loop(0, pairs - 1, far, 0)
        chunk(mine)
        exchange(kind, result.at[rows(partner), :], landing.at[me], partner, me).start()
        landing[me] = result[rows(me), :]

    convolved(2, wch, mch, mseq)

    others(-1, lambda source: exchange(
        1, usend.at[source], uch.at[rows(source), :], source, source).wait_recv())

    def make_products(tile, carry):
        here = wide(tile)
        spec = jnp.dot(ahead[here, :], uch[...], preferred_element_type=f32)
        x_re, x_im = spec[:ROWS], spec[ROWS:]
        for left, target in ((kspec, prod), (wspec, corr)):
            l_re, l_im = left[here, :][:ROWS], left[here, :][ROWS:]
            target[here, :] = jnp.concatenate(
                [l_re * x_re + l_im * x_im, l_re * x_im - l_im * x_re], axis=0
            ).astype(bf16)
        return carry

    lax.fori_loop(0, shards, make_products, 0)
    convolved(3, uch, gch, gseq)

    def pass_mixed(source):
        block = mseq[source].astype(f32)
        stage[0, source] = (g2[:, cols(source)].astype(f32) * block).astype(bf16)
        stage[1, source] = (og[:, cols(source)].astype(f32) * block).astype(bf16)
        handed(0, source).start()
        handed(1, source).start()

    def land_mixed(source):
        exchange(2, mch.at[rows(source), :], mseq.at[source], source, source).wait_recv()
        pass_mixed(source)

    pass_mixed(me)
    others(-1, land_mixed)

    def correlate(tile, carry):
        here = wide(tile)
        step = (lax.broadcasted_iota(jnp.int32, (PAIR, 1), 0) + tile * PAIR).astype(f32)
        grad = jnp.dot(back[here, :], corr[...], preferred_element_type=f32)
        graw[here, :] = (grad * env[here, :]).astype(bf16)
        sum_d, sum_s = carry
        sum_d += jnp.sum(grad * kf[here, :] * (-step / length), axis=0, keepdims=True)
        both = uch[here, :].astype(f32) * wch[here, :].astype(f32)
        return sum_d, sum_s + jnp.sum(both, axis=0, keepdims=True)

    empty = jnp.zeros((1, width), f32)
    sum_d, sum_s = lax.fori_loop(0, length // PAIR, correlate, (empty, empty))
    o_decay[...] = sum_d
    o_skip[...] = sum_s

    def halves(value):
        top = value.astype(bf16)
        return jnp.concatenate([top, (value - top.astype(f32)).astype(bf16)], axis=0)

    preact = jnp.dot(wext_t[...], feat[...], precision=high)
    both = jnp.dot(halves(jnp.sin(preact)), graw[...], preferred_element_type=f32)
    o_wf[...] = both[:hidden] + both[hidden:]
    both = lax.dot_general(
        halves(wf[...]), graw[...], (((1,), (1,)), ((), ())), preferred_element_type=f32
    )
    grad_pre = (both[:hidden] + both[hidden:]) * jnp.cos(preact)
    part[...] = lax.dot_general(
        feat[...], jnp.concatenate([grad_pre, jnp.zeros_like(grad_pre)], axis=0),
        (((1,), (1,)), ((), ())), precision=high,
    )
    others(1, lambda there: shared(there, me).start())

    def pass_grad(source):
        block = gseq[source].astype(f32)
        stage[2, source] = (g1[:, cols(source)].astype(f32) * block).astype(bf16)
        stage[3, source] = (v[:, cols(source)].astype(f32) * block).astype(bf16)
        handed(2, source).start()
        handed(3, source).start()

    def land_grad(source):
        exchange(3, gch.at[rows(source), :], gseq.at[source], source, source).wait_recv()
        pass_grad(source)

    pass_grad(me)
    others(-1, land_grad)

    parts[me] = part[...]
    others(-1, lambda source: shared(source, source).wait_recv())
    total = parts[0]
    for index in range(1, shards):
        total = total + parts[index]
    o_emb[...] = total

    def sent(there):
        exchange(1, usend.at[there], uch.at[rows(me), :], there, me).wait_send()
        exchange(2, mch.at[rows(there), :], mseq.at[me], there, me).wait_send()
        exchange(3, gch.at[rows(there), :], gseq.at[me], there, me).wait_send()
        shared(there, me).wait_send()

    others(1, sent)

    def finish(slot, carry):
        for kind in range(4):
            handed(kind, slot).wait()
        return carry

    lax.fori_loop(0, shards, finish, 0)


CHUNKS = 4


def finish_kernel(
    a_in, b_in, c_in, d_in, emb, wf, row_d, row_s,
    a_out, b_out, c_out, d_out, o_emb, o_bias, o_wf, o_d, o_s, held, got, put,
):
    rows = ROWS // CHUNKS
    reads, writes = [], []
    for kind, (src, dst) in enumerate(
        ((a_in, a_out), (b_in, b_out), (c_in, c_out), (d_in, d_out))
    ):
        for chunk in range(CHUNKS):
            here = pl.ds(chunk * rows, rows)
            index = kind * CHUNKS + chunk
            middle = held.at[kind, here, :]
            reads.append(pltpu.make_async_copy(src.at[here, :], middle, got.at[index]))
            writes.append(pltpu.make_async_copy(middle, dst.at[0, here, :], put.at[index]))
    for read in reads:
        read.start()
    o_emb[0] = emb[:E, : o_emb.shape[2]]
    o_bias[...] = emb[E : E + 1, : o_bias.shape[1]]
    o_wf[0] = wf[...]
    o_d[...] = row_d[...]
    o_s[...] = row_s[...]
    for read, write in zip(reads, writes):
        read.wait()
        write.start()
    for write in writes:
        write.wait()


def fused_section(v, g1, g2, og, w_embed, b_embed, wf, decay, skip):
    shards = lax.axis_size("seq")
    pipes = lax.axis_size("pipe")
    length = shards * ROWS
    wide_cols = v.shape[1]
    width = wf.shape[1]
    hidden = wf.shape[0]
    f32, bf16 = jnp.float32, jnp.bfloat16
    feat = padded_features(length)
    tables = split_tables(length)
    vmem = pl.BlockSpec(memory_space=pltpu.VMEM)
    hbm = pl.BlockSpec(memory_space=pl.ANY)
    stream = jax.ShapeDtypeStruct((ROWS, wide_cols), bf16)
    row = jax.ShapeDtypeStruct((1, width), f32)
    dma = pltpu.SemaphoreType.DMA
    results = pl.pallas_call(
        functools.partial(section_kernel, shards, pipes),
        out_shape=(
            stream, stream, stream, stream,
            jax.ShapeDtypeStruct((PADDED, 2 * hidden), f32),
            jax.ShapeDtypeStruct((hidden, width), f32), row, row,
        ),
        in_specs=[hbm] * 14 + [vmem] * 5,
        out_specs=(hbm,) * 4 + (vmem,) * 4,
        scratch_shapes=[
            pltpu.VMEM((2 * length, length), bf16),
            pltpu.VMEM((length, 2 * length), bf16),
            pltpu.VMEM((length, width), bf16),
            pltpu.VMEM((length, width), f32),
            pltpu.VMEM((length, width), f32),
            pltpu.VMEM((2 * length, width), f32),
            pltpu.VMEM((2 * length, width), f32),
            pltpu.VMEM((2 * length, width), bf16),
            pltpu.VMEM((2 * length, width), bf16),
            pltpu.VMEM((length, width), bf16),
            pltpu.VMEM((shards, ROWS, width), bf16),
            pltpu.VMEM((shards, ROWS, width), bf16),
            pltpu.VMEM((length, width), bf16),
            pltpu.VMEM((length, width), bf16),
            pltpu.VMEM((length, width), bf16),
            pltpu.VMEM((length, width), bf16),
            pltpu.VMEM((shards, ROWS, width), bf16),
            pltpu.VMEM((shards, ROWS, width), bf16),
            pltpu.VMEM((4, shards, ROWS, width), bf16),
            pltpu.VMEM((PADDED, 2 * hidden), f32),
            pltpu.VMEM((shards, PADDED, 2 * hidden), f32),
            *[pltpu.VMEM((ROWS, wide_cols), bf16)] * 4,
            pltpu.VMEM((length, PADDED), f32),
            *[pltpu.VMEM((ROWS, length), f32)] * 2,
            *[pltpu.VMEM((shards, length), f32)] * 2,
            *[pltpu.VMEM((ROWS, length), f32)] * 2,
            *[pltpu.VMEM((shards, length), f32)] * 2,
            pltpu.VMEM((PADDED, length), f32),
            pltpu.VMEM((hidden, PADDED), f32),
            dma((14,)),
            dma((4, shards)), dma((4, shards)),
            dma((4, shards)), dma((4, shards)),
            dma((shards,)), dma((shards,)),
        ],
        compiler_params=pltpu.CompilerParams(
            collective_id=0, has_side_effects=True, vmem_limit_bytes=60 * 1024 * 1024
        ),
    )(
        v, g1, g2, og, jnp.asarray(feat), jnp.asarray(feat.T.copy()), *tables,
        wf, decay[None], skip[None], w_embed.T, b_embed[None],
    )
    final = jax.ShapeDtypeStruct((1, ROWS, wide_cols), bf16)
    return tuple(
        pl.pallas_call(
            finish_kernel,
            out_shape=(
                final, final, final, final,
                jax.ShapeDtypeStruct((1, E, hidden), f32),
                jax.ShapeDtypeStruct((1, hidden), f32),
                jax.ShapeDtypeStruct((1, hidden, width), f32), row, row,
            ),
            in_specs=[hbm] * 4 + [vmem] * 4,
            out_specs=(hbm,) * 4 + (vmem,) * 5,
            scratch_shapes=[
                pltpu.VMEM((4, ROWS, wide_cols), bf16),
                dma((4 * CHUNKS,)), dma((4 * CHUNKS,)),
            ],
            compiler_params=pltpu.CompilerParams(vmem_limit_bytes=60 * 1024 * 1024),
        )(*results)
    )


def spectral_product(left, right, conjugate_left):
    left_re = left[0]
    left_im = left[1]
    right_re = right[0]
    right_im = right[1]
    if conjugate_left:
        left_im = -left_im
    return jnp.stack(
        [left_re * right_re - left_im * right_im, left_re * right_im + left_im * right_re], axis=0
    )


def per_device(value_in, gate_one, gate_two, out_grad, w_embed, b_embed, w_filter, decay, skip):
    values = value_in[0]
    gate_first = gate_one[0]
    gate_second = gate_two[0]
    cotangent = out_grad[0]
    filter_w = w_filter[0]
    shards = lax.axis_size("seq")
    length = values.shape[0] * shards
    if length <= 1024 and values.shape[0] == ROWS and shards % 2 == 0 and lax.axis_size("pipe") > 2:
        return fused_section(
            values, gate_first, gate_second, cotangent,
            w_embed[0], b_embed[0], filter_w, decay[0], skip[0],
        )
    weighted = (values.astype(jnp.float32) * gate_first.astype(jnp.float32)).astype(jnp.bfloat16)
    upstream = (cotangent.astype(jnp.float32) * gate_second.astype(jnp.float32)).astype(
        jnp.bfloat16
    )
    features = position_features(length)
    preact = contract("ef,et->ft", w_embed[0], features) + b_embed[0][:, None]
    activation = jnp.sin(preact)
    positions = jnp.arange(length, dtype=jnp.int32).astype(jnp.float32)[:, None]
    envelope = jnp.exp(-decay[0][None, :] * positions / length) * (1.0 / math.sqrt(length))
    kernel = contract("ft,fc->tc", activation, filter_w) * envelope
    tables_all = build_tables(length)
    forward_transform, inverse_transform = staged_forward, staged_inverse
    kernel_spec = forward_transform(kernel, tables_all)
    skip_row = skip[0][None, :]
    weighted_chan, upstream_chan = (
        lax.all_to_all(weighted, "seq", split_axis=1, concat_axis=0, tiled=True),
        lax.all_to_all(upstream, "seq", split_axis=1, concat_axis=0, tiled=True),
    )
    weighted_f = weighted_chan.astype(jnp.float32)
    weighted_spec = forward_transform(weighted_f, tables_all)
    conv = inverse_transform(spectral_product(kernel_spec, weighted_spec, False), tables_all)
    mixed_chan, weighted_f, weighted_spec = (
        (conv + skip_row * weighted_f).astype(jnp.bfloat16),
        weighted_f,
        weighted_spec,
    )
    upstream_f = upstream_chan.astype(jnp.float32)
    upstream_spec = forward_transform(upstream_f, tables_all)
    backward_conv = inverse_transform(
        spectral_product(kernel_spec, upstream_spec, True), tables_all
    )
    grad_chan = (backward_conv + skip_row * upstream_f).astype(jnp.bfloat16)
    grad_skip = jnp.sum(upstream_f * weighted_f, axis=0)
    grad_kernel = inverse_transform(
        spectral_product(weighted_spec, upstream_spec, True), tables_all
    )
    grad_chan, grad_skip, grad_kernel = (grad_chan, grad_skip, grad_kernel)
    mixed_seq, grad_weighted = (
        lax.all_to_all(mixed_chan, "seq", split_axis=0, concat_axis=1, tiled=True),
        lax.all_to_all(grad_chan, "seq", split_axis=0, concat_axis=1, tiled=True),
    )
    output = (gate_second.astype(jnp.float32) * mixed_seq.astype(jnp.float32)).astype(jnp.bfloat16)
    next_input = from_behind(output, "pipe", 1)
    grad_decay = jnp.sum(grad_kernel * kernel * (-positions / length), axis=0)
    grad_raw = grad_kernel * envelope
    grad_filter_w = contract("ft,tc->fc", activation, grad_raw)
    grad_preact = contract("fc,tc->ft", filter_w, grad_raw) * jnp.cos(preact)
    part_weight = contract("et,ft->ef", features, grad_preact)
    part_bias = jnp.sum(grad_preact, axis=1)
    grad_embed_w, grad_embed_b = lax.psum((part_weight, part_bias), "seq")
    grad_values = (grad_weighted.astype(jnp.float32) * gate_first.astype(jnp.float32)).astype(
        jnp.bfloat16
    )
    grad_first = (grad_weighted.astype(jnp.float32) * values.astype(jnp.float32)).astype(
        jnp.bfloat16
    )
    grad_second = (cotangent.astype(jnp.float32) * mixed_seq.astype(jnp.float32)).astype(
        jnp.bfloat16
    )
    moved_values, moved_first, moved_second = from_behind(
        (grad_values, grad_first, grad_second), "pipe", -1
    )
    return (
        next_input[None],
        moved_values[None],
        moved_first[None],
        moved_second[None],
        grad_embed_w[None],
        grad_embed_b[None],
        grad_filter_w[None],
        grad_decay[None],
        grad_skip[None],
    )


def solution(mesh):
    return jax.shard_map(
        per_device,
        mesh=mesh,
        in_specs=(
            P("pipe", "seq", None),
            P("pipe", "seq", None),
            P("pipe", "seq", None),
            P("pipe", "seq", None),
            P("pipe", None, None),
            P("pipe", None),
            P("pipe", None, "seq"),
            P("pipe", "seq"),
            P("pipe", "seq"),
        ),
        out_specs=(
            P("pipe", "seq", None),
            P("pipe", "seq", None),
            P("pipe", "seq", None),
            P("pipe", "seq", None),
            P("pipe", None, None),
            P("pipe", None),
            P("pipe", None, "seq"),
            P("pipe", "seq"),
            P("pipe", "seq"),
        ),
        check_vma=False,
    )
```
